256 devices in a mesh: seq: 32 (over x, z), tp: 8 (over y, core).
Axes of the slice: x: 4, y: 4, z: 8, core: 2. Of those that a mesh axis runs over, the one named last changes fastest.
Arguments:
- tokens: bfloat16 [16384, 5376], P('seq'), may hold values from -6 to 6
- query_weight: bfloat16 [5376, 2048], P(None, 'tp')
- key_weight: bfloat16 [5376, 1024], P(None, 'tp')
- value_weight: bfloat16 [5376, 1024], P(None, 'tp'), may hold values from -0.078125 to 0.078125
- query_norm_gain: float32 [128], replicated, as said below
- key_norm_gain: float32 [128], replicated, as said below
- adapter_down_weight: bfloat16 [32, 5376, 64], P('seq', 'tp'), may hold values from -0.078125 to 0.078125
- adapter_up_weight: bfloat16 [32, 64, 2048], P('seq', None, 'tp'), may hold values from -0.75 to 0.75
- token_adapter_index: int32 [16384, 1], P('seq'), may hold values from 0 to 31; in each aligned block of 512 rows (0 to 511, 512 to 1023, ...) at most 32 rows name the same one
- packed_prompt_length: int32 [16], replicated, may hold values from 1 to 2048, 16384 in all
Outputs:
- attended: bfloat16 [16384, 2048], P('seq', 'tp')
The draws below stay inside these ranges and needn't reach their ends.
Inputs may be any that keep to these rules, and one draw needn't show every extreme that they name: `token_adapter_index`: in each aligned block of 512 rows (the rows of one index of seq) no adapter is named by more than 32 rows, a bound that some block reaches. `packed_prompt_length`: they sum to 16384; the largest is exactly 2048. `query_norm_gain`: positive gains. `key_norm_gain`: positive gains.
All inputs are finite; a program needn't handle non-finite values.
Results may differ from the reference program's by a relative error of at most 0.02.
Values may be sent and summed in bfloat16 or wider, within the bound.
No kernel may reach another device: no remote copies, remote signals or barrier semaphores. Data moves between devices by JAX's collectives and lax.ppermute only.
A program may use at most 64 MiB of HBM per device.

```python
import math
import jax
import jax.numpy as jnp
import numpy as np
from jax import lax

MODEL_WIDTH = 5376
HEAD_SIZE = 128
WINDOW = 1024
QUERY_HEADS = 16
KV = 8
ADAPTER_RANK = 64
TOK_DEV = 512
SLAB_TOKENS = 16384
ADAPTER_COUNT = 32
CAP = 32
COUNT = 16
N_SEQ = 32


def base_query(key):
    raw = jnp.clip(jax.random.normal(jax.random.fold_in(key, 7), (MODEL_WIDTH, QUERY_HEADS * HEAD_SIZE), jnp.float32), -6.0, 6.0)
    return raw * MODEL_WIDTH ** (-0.5)


def draw_query_weight(key, part):
    return base_query(key).astype(jnp.bfloat16)


def draw_key_weight(key, part):
    raw = jnp.clip(jax.random.normal(jax.random.fold_in(key, 11), (MODEL_WIDTH, KV * HEAD_SIZE), jnp.float32), -6.0, 6.0)
    return (raw * MODEL_WIDTH ** (-0.5)).astype(jnp.bfloat16)


def draw_query_norm_gain(key, part):
    return jnp.exp(jax.random.uniform(jax.random.fold_in(key, 21), (HEAD_SIZE,), jnp.float32, math.log(0.5), math.log(2.0)))


def draw_key_norm_gain(key, part):
    return jnp.exp(jax.random.uniform(jax.random.fold_in(key, 23), (HEAD_SIZE,), jnp.float32, math.log(0.5), math.log(2.0)))


def block_levels(key, dims, pieces, smallest, high):
    factor_of, own = 1.0, jax.random.fold_in(key, 6)
    for axis_at, parts in pieces:
        draws = jnp.exp(jax.random.uniform(jax.random.fold_in(own, axis_at), (parts,), jnp.float32, smallest / len(pieces), high / len(pieces)))
        factor_of = factor_of * jnp.repeat(draws, dims[axis_at] // parts).reshape([-1 if axis == axis_at else 1 for axis in range(len(dims))])
    return factor_of


def length_profile(amount, total, bound, lean):
    portions = [(1 << 20) // math.isqrt(grade ** lean) + 1 for grade in range(2, amount + 1)]
    spare, given = total - bound - (amount - 1), [1] * (amount - 1)
    while spare > 0:
        candidates = [i for i in range(amount - 1) if given[i] < bound]
        mass, left = sum([portions[i] for i in candidates]), spare
        for i in candidates:
            more = min(bound - given[i], max(1, left * portions[i] // mass), spare)
            given[i] = given[i] + more
            spare = spare - more
    return np.array([bound] + given)


def uneven_parts(stream_key, amount, total, bound, slope):
    if amount == 2:
        one = jax.random.randint(stream_key, (), max(1, total - bound), min(bound, total - 1) + 1)
        return jnp.stack([one, total - one])
    sizes = jnp.asarray(length_profile(amount, total, bound, slope), jnp.int32)
    couples = (amount - 1) // 2
    donor, receiver = sizes[1:1 + 2 * couples:2], sizes[2:2 + 2 * couples:2]
    margin = jnp.minimum(donor - 1, bound - receiver)
    moved = jax.random.randint(jax.random.fold_in(stream_key, 1), (couples,), 0, 1 << 20) % (margin + 1)
    sizes = sizes.at[1:1 + 2 * couples:2].set(donor - moved).at[2:2 + 2 * couples:2].set(receiver + moved)
    return sizes[jax.random.permutation(jax.random.fold_in(stream_key, 2), amount)]


def shared_out(own_key, own, number, rows, number_of, top, bound, lean):
    ranking = jax.random.permutation(own_key, number_of)
    crowded, ordinary = shares(number_of, rows * top, bound, lean, True), shares(number_of, rows * top, bound, lean, False)
    places = jnp.arange(number_of)

    def named(lengths, turn):
        used = int((lengths > 0).sum())
        fixed = max(1, used // 4)
        shifted = fixed + (places - fixed + turn * (used - fixed)) % max(1, number_of - fixed)
        return jnp.zeros((number_of,), jnp.int32).at[ranking[jnp.where(places < fixed, places, shifted)]].set(jnp.asarray(lengths, jnp.int32))

    lengths = jnp.where(number % 4 == 0, named(crowded, number // 4), named(ordinary, number - number // 4 - 1))
    mixed = jax.random.permutation(jax.random.fold_in(own, 3), number_of)
    source_of, receiver = mixed[0:number_of // 2 * 2:2], mixed[1:number_of // 2 * 2:2]
    slack = jnp.minimum(lengths[source_of] - 1, bound - lengths[receiver]) // 2
    slack = jnp.where((source_of == ranking[0]) | (receiver == ranking[0]) | (lengths[receiver] == 0), 0, jnp.maximum(slack, 0))
    shifted = jax.random.randint(jax.random.fold_in(own, 4), (number_of // 2,), 0, 1 << 20) % (slack + 1)
    lengths = lengths.at[source_of].add(-shifted).at[receiver].add(shifted)
    labels = jnp.searchsorted(jnp.cumsum(lengths), jnp.arange(rows * top), side="right").astype(jnp.int32)
    listing = labels.reshape(top, rows).T
    listing = listing[jax.random.permutation(jax.random.fold_in(own, 1), rows)]
    turn = jax.random.randint(jax.random.fold_in(own, 2), (rows, 1), 0, top)
    return jnp.take_along_axis(listing, (jnp.arange(top)[None, :] + turn) % top, axis=1)


def shares(amount, total, bound, slope, full):
    weights = [(1 << 20) // math.isqrt(rank ** slope) + 1 for rank in range(1, amount + 1)]
    largest = bound if full else min(bound, max(-(-total // amount), total * weights[0] // sum(weights)))
    least = 1 if total - largest >= amount - 1 else 0
    holding, spare = [largest] + [least] * (amount - 1), total - largest - least * (amount - 1)
    while spare > 0:
        movable = [i for i in range(1, amount) if holding[i] < largest] or [i for i in range(1, amount) if holding[i] < bound]
        mass, budget = sum([weights[i] for i in movable]), spare
        for i in movable:
            extra = min(bound - holding[i], max(1, budget * weights[i] // mass), spare)
            holding[i] = holding[i] + extra
            spare = spare - extra
    return np.array(holding)


def noise(key, dims, scale, limit, pieces=(), held_as=jnp.bfloat16):
    entries = scale * jax.random.normal(key, dims, jnp.float32)
    if pieces:
        entries = entries * block_levels(key, dims, pieces, -0.22, 0.18)
    return jnp.clip(entries, -limit, limit).astype(held_as)


def setup_inputs(seed: int = 0) -> dict:
    key_of = jax.random.split(jax.random.key(seed), 11)
    tokens = noise(key_of[0], (SLAB_TOKENS, MODEL_WIDTH), 1.0, 6.0, ((0, 32),))
    query_weight = draw_query_weight(jax.random.fold_in(key_of[10], 71), 0)
    key_weight = draw_key_weight(jax.random.fold_in(key_of[10], 71), 0)
    value_weight = noise(key_of[3], (MODEL_WIDTH, KV * HEAD_SIZE), MODEL_WIDTH ** -0.5, 0.078125, ((1, 8),))
    query_norm_gain = draw_query_norm_gain(jax.random.fold_in(key_of[10], 71), 0)
    key_norm_gain = draw_key_norm_gain(jax.random.fold_in(key_of[10], 71), 0)
    adapter_down_weight = noise(key_of[6], (ADAPTER_COUNT, MODEL_WIDTH, ADAPTER_RANK), MODEL_WIDTH ** -0.5, 0.078125, ((0, 32), (1, 8)))
    adapter_up_weight = noise(key_of[7], (ADAPTER_COUNT, ADAPTER_RANK, QUERY_HEADS * HEAD_SIZE), ADAPTER_RANK ** -0.5, 0.75, ((0, 32), (2, 8)))
    token_adapter_index_keys = jax.random.split(jax.random.fold_in(key_of[8], 1), SLAB_TOKENS // TOK_DEV)
    token_adapter_index_turns = jax.random.permutation(jax.random.fold_in(key_of[8], 3), SLAB_TOKENS // TOK_DEV)
    token_adapter_index = jax.vmap(lambda own, number: shared_out(jax.random.fold_in(key_of[8], 2), own, number, TOK_DEV, ADAPTER_COUNT, 1, CAP, 2))(token_adapter_index_keys, token_adapter_index_turns).reshape((SLAB_TOKENS, 1))
    packed_prompt_length = uneven_parts(key_of[9], COUNT, SLAB_TOKENS, 4 * TOK_DEV, 2).astype(jnp.int32)
    return dict(tokens=tokens, query_weight=query_weight, key_weight=key_weight, value_weight=value_weight, query_norm_gain=query_norm_gain, key_norm_gain=key_norm_gain, adapter_down_weight=adapter_down_weight, adapter_up_weight=adapter_up_weight, token_adapter_index=token_adapter_index, packed_prompt_length=packed_prompt_length)


query_scale = 0.07715167498104596

def make_dispatch(adapter_of, adapter_total, capacity):
    one_hot = (adapter_of[:, None] == jnp.arange(adapter_total, dtype=jnp.int32)[None, :]).astype(jnp.int32)
    before = jnp.cumsum(one_hot, axis=0) - one_hot
    slot_index = lax.optimization_barrier(jnp.sum(before * one_hot, axis=1))
    target = adapter_of * capacity + slot_index
    return (jnp.arange(adapter_total * capacity, dtype=jnp.int32)[:, None] == target[None, :]).astype(jnp.bfloat16)

def normalize(field, gain):
    return field / jnp.sqrt(lax.optimization_barrier(jnp.mean(field * field, axis=-1, keepdims=True)) + 1e-06) * gain

def rotate(field, positions):
    half = field.shape[-1] // 2
    freq = jnp.exp(-(2.0 * jnp.arange(half, dtype=jnp.float32) / field.shape[-1]) * jnp.log(jnp.float32(10000.0)))
    angle = positions[:, None] * freq[None, :]
    cosine = jnp.cos(angle)[:, None, :]
    sine = jnp.sin(angle)[:, None, :]
    first = field[..., :half]
    second = field[..., half:]
    return jnp.concatenate([first * cosine - second * sine, second * cosine + first * sine], axis=-1)

def reference(tokens, query_weight, key_weight, value_weight, query_norm_gain, key_norm_gain, adapter_down_weight, adapter_up_weight, token_adapter_index, packed_prompt_length):
    adapter_total = adapter_down_weight.shape[0]
    down_projected_wide = adapter_down_weight.astype(jnp.float32)
    up_projected_wide = adapter_up_weight.astype(jnp.float32)

    def adapter_block(token_block):
        begin = (token_block * TOK_DEV).astype(jnp.int32)
        rows_x = lax.dynamic_slice_in_dim(tokens, begin, TOK_DEV, 0)
        adapter_of = lax.dynamic_slice_in_dim(token_adapter_index[:, 0], begin, TOK_DEV, 0)
        dispatch = make_dispatch(adapter_of, adapter_total, CAP)
        packed = jnp.dot(dispatch, rows_x, preferred_element_type=jnp.float32).astype(jnp.bfloat16)
        packed = packed.reshape(adapter_total, CAP, MODEL_WIDTH).astype(jnp.float32)
        low_rank = jnp.einsum('acd,adr->acr', packed, down_projected_wide).astype(jnp.bfloat16)
        delta_slots = jnp.einsum('acr,are->ace', low_rank.astype(jnp.float32), up_projected_wide).astype(jnp.bfloat16)
        delta_slots = delta_slots.reshape(adapter_total * CAP, QUERY_HEADS * HEAD_SIZE)
        return jnp.einsum('st,se->te', dispatch.astype(jnp.float32), delta_slots.astype(jnp.float32))
    query_delta = lax.map(adapter_block, jnp.arange(N_SEQ, dtype=jnp.int32)).reshape(SLAB_TOKENS, QUERY_HEADS * HEAD_SIZE)
    query = jnp.dot(tokens, query_weight, preferred_element_type=jnp.float32) + query_delta
    keys = jnp.dot(tokens, key_weight, preferred_element_type=jnp.float32)
    values = jnp.dot(tokens, value_weight, preferred_element_type=jnp.float32).astype(jnp.bfloat16)
    positions = jnp.arange(SLAB_TOKENS, dtype=jnp.int32)
    pos_float = positions.astype(jnp.float32)
    query_rot = rotate(normalize(query.reshape(SLAB_TOKENS, QUERY_HEADS, HEAD_SIZE), query_norm_gain), pos_float).astype(jnp.bfloat16)
    key_rot = rotate(normalize(keys.reshape(SLAB_TOKENS, KV, HEAD_SIZE), key_norm_gain), pos_float).astype(jnp.bfloat16)
    key_pad = jnp.pad(key_rot, ((WINDOW, 0), (0, 0), (0, 0)))
    value_pad = jnp.pad(values.reshape(SLAB_TOKENS, KV, HEAD_SIZE), ((WINDOW, 0), (0, 0), (0, 0)))
    starts = jnp.cumsum(packed_prompt_length) - packed_prompt_length
    groups = QUERY_HEADS // KV

    def attend_block(token_block):
        begin = (token_block * TOK_DEV).astype(jnp.int32)
        query_part = lax.dynamic_slice_in_dim(query_rot, begin, TOK_DEV, 0).reshape(TOK_DEV, KV, groups, HEAD_SIZE)
        key_part = lax.dynamic_slice_in_dim(key_pad, begin, WINDOW + TOK_DEV, 0)
        value_part = lax.dynamic_slice_in_dim(value_pad, begin, WINDOW + TOK_DEV, 0)
        query_pos = begin + jnp.arange(TOK_DEV, dtype=jnp.int32)
        key_pos = begin - WINDOW + jnp.arange(WINDOW + TOK_DEV, dtype=jnp.int32)
        prompt_start = lax.optimization_barrier(jnp.max(jnp.where(starts[None, :] <= query_pos[:, None], starts[None, :], 0), axis=1))
        lower = jnp.maximum(query_pos - WINDOW + 1, prompt_start)
        allowed = (key_pos[None, :] >= lower[:, None]) & (key_pos[None, :] <= query_pos[:, None])
        scores = jnp.einsum('tkgd,skd->kgts', query_part.astype(jnp.float32), key_part.astype(jnp.float32)) * query_scale
        scores = jnp.where(allowed[None, None], scores, jnp.float32(-1e+30))
        peak = lax.optimization_barrier(jnp.max(scores, axis=-1, keepdims=True))
        weights = jnp.exp(scores - peak)
        probs = (weights / lax.optimization_barrier(jnp.sum(weights, axis=-1, keepdims=True))).astype(jnp.bfloat16)
        mixed = jnp.einsum('kgts,skd->tkgd', probs.astype(jnp.float32), value_part.astype(jnp.float32))
        return mixed.astype(jnp.bfloat16).reshape(TOK_DEV, QUERY_HEADS * HEAD_SIZE)
    attended = lax.map(attend_block, jnp.arange(N_SEQ, dtype=jnp.int32))
    return attended.reshape(SLAB_TOKENS, QUERY_HEADS * HEAD_SIZE)
```

```python
import functools
import jax
import jax.numpy as jnp
from jax import lax
from jax.experimental import pallas as pl
from jax.experimental.pallas import tpu as pltpu
from jax.sharding import Mesh, PartitionSpec as P

WINDOW = 1024
QUERY_SCALE = 0.07715167498104596
X, Z, T = 4, 8, 8
ROWS, WIDTH, HEAD, RANK, CAP = 512, 5376, 128, 64, 32
SLICE = WIDTH // T
PAD = 768
STEP = 768
STEPS = WIDTH // STEP
UP = 256
SLOTS = X * T * CAP


def dot(a, b, ca=1, cb=0):
    return lax.dot_general(a, b, (((ca,), (cb,)), ((), ())), preferred_element_type=jnp.float32)


def pack_kernel(idx_ref, x_ref, out0, out1, out2, out3, target_ref, pick):
    x, t = lax.axis_index("x"), lax.axis_index("tp")

    @pl.when(pl.program_id(0) == 0)
    def _():
        idx = idx_ref[...]
        named = lax.broadcasted_iota(jnp.int32, (X * T, ROWS), 0) == idx
        earlier = lax.broadcasted_iota(jnp.int32, (ROWS, ROWS), 0) < lax.broadcasted_iota(
            jnp.int32, (ROWS, ROWS), 1
        )
        before = dot(named.astype(jnp.float32).astype(jnp.bfloat16),
                     earlier.astype(jnp.float32).astype(jnp.bfloat16))
        rank = jnp.sum(jnp.where(named, before, 0.0), axis=0, keepdims=True).astype(jnp.int32)
        target = idx * CAP + rank
        target_ref[...] = target
        slot = lax.broadcasted_iota(jnp.int32, (CAP, ROWS), 0)
        for d in range(X):
            adapter = lax.rem(x + d, X) * T + t
            pick[d * CAP:(d + 1) * CAP, :] = (
                (slot + adapter * CAP == target).astype(jnp.float32).astype(jnp.bfloat16)
            )

    packed = dot(pick[...], x_ref[...]).astype(jnp.bfloat16)
    for d, out in enumerate((out0, out1, out2, out3)):
        out[...] = packed[d * CAP:(d + 1) * CAP, :]


def pack(idx, tokens):
    row = jax.ShapeDtypeStruct((CAP, WIDTH), jnp.bfloat16)
    return pl.pallas_call(
        pack_kernel,
        grid=(STEPS,),
        in_specs=[
            pl.BlockSpec((1, ROWS), lambda j: (0, 0)),
            pl.BlockSpec((ROWS, STEP), lambda j: (0, j)),
        ],
        out_specs=[pl.BlockSpec((CAP, STEP), lambda j: (0, j))] * X
        + [pl.BlockSpec((1, ROWS), lambda j: (0, 0))],
        out_shape=[row] * X + [jax.ShapeDtypeStruct((1, ROWS), jnp.int32)],
        scratch_shapes=[pltpu.VMEM((X * CAP, ROWS), jnp.bfloat16)],
        cost_estimate=pl.CostEstimate(
            flops=2 * X * CAP * ROWS * WIDTH, bytes_accessed=7_000_000, transcendentals=0
        ),
        name="pack",
    )(idx, tokens)


def unit(field, gain):
    return field / jnp.sqrt(jnp.mean(field * field, axis=-1, keepdims=True) + 1e-06) * gain


def turn(field, cosine, sine):
    return field * cosine + pltpu.roll(field, HEAD // 2, 1) * sine


def project_kernel(
    lens_ref, x_ref, wq_ref, wk_ref, wv_ref, cos_ref, sin_ref, gain_ref, target_ref,
    q_ref, kv_ref, lower_ref, column_ref, acc_q, acc_kv,
):
    j = pl.program_id(0)
    q = dot(x_ref[...], wq_ref[...])
    kv = dot(x_ref[...], jnp.concatenate([wk_ref[...], wv_ref[...]], axis=1))

    @pl.when(j == 0)
    def _():
        acc_q[...] = q
        acc_kv[...] = kv
        begin = (lax.axis_index("x") * Z + lax.axis_index("z")) * ROWS
        place = begin + lax.broadcasted_iota(jnp.int32, (ROWS, HEAD), 0)
        start = jnp.zeros((ROWS, HEAD), jnp.int32)
        at = jnp.int32(0)
        for i in range(lens_ref.shape[0]):
            start = jnp.where(place >= at, at, start)
            at = at + lens_ref[i]
        lower_ref[...] = jnp.maximum(start, place - (WINDOW - 1)) - (begin - WINDOW)
        wide = jnp.broadcast_to(target_ref[...].astype(jnp.float32), (HEAD, ROWS))
        column_ref[...] = jnp.transpose(wide).astype(jnp.int32)

    @pl.when(j > 0)
    def _():
        acc_q[...] += q
        acc_kv[...] += kv

    @pl.when(j == STEPS - 1)
    def _():
        q_ref[...] = acc_q[...]
        key = turn(unit(acc_kv[:, :HEAD], gain_ref[...]), cos_ref[...], sin_ref[...])
        kv_ref[:, :HEAD] = key.astype(jnp.bfloat16)
        kv_ref[:, HEAD:] = acc_kv[:, HEAD:].astype(jnp.bfloat16)


def project(lens, tokens, wq, wk, wv, cosine, sine, gain, target):
    fixed = lambda shape: pl.BlockSpec(shape, lambda j: (0, 0))
    return pl.pallas_call(
        project_kernel,
        grid=(STEPS,),
        in_specs=[
            pl.BlockSpec(memory_space=pltpu.SMEM),
            pl.BlockSpec((ROWS, STEP), lambda j: (0, j)),
            pl.BlockSpec((STEP, 2 * HEAD), lambda j: (j, 0)),
            pl.BlockSpec((STEP, HEAD), lambda j: (j, 0)),
            pl.BlockSpec((STEP, HEAD), lambda j: (j, 0)),
            fixed((ROWS, HEAD)), fixed((ROWS, HEAD)), fixed((1, HEAD)), fixed((1, ROWS)),
        ],
        out_specs=[fixed((ROWS, 2 * HEAD)), fixed((ROWS, 2 * HEAD)),
                   fixed((ROWS, HEAD)), fixed((ROWS, HEAD))],
        out_shape=[
            jax.ShapeDtypeStruct((ROWS, 2 * HEAD), jnp.float32),
            jax.ShapeDtypeStruct((ROWS, 2 * HEAD), jnp.bfloat16),
            jax.ShapeDtypeStruct((ROWS, HEAD), jnp.int32),
            jax.ShapeDtypeStruct((ROWS, HEAD), jnp.int32),
        ],
        scratch_shapes=[pltpu.VMEM((ROWS, 2 * HEAD), jnp.float32)] * 2,
        cost_estimate=pl.CostEstimate(
            flops=2 * ROWS * WIDTH * 512, bytes_accessed=12_500_000, transcendentals=0
        ),
        name="project",
    )(lens, tokens, wq, wk, wv, cosine, sine, gain, target)


def adapt_kernel(*refs):
    rows, weights, out, held, low_ref = refs[:X], refs[X:X + T], refs[X + T], refs[-2], refs[-1]
    x, z = lax.axis_index("x"), lax.axis_index("z")
    for d in range(T):
        held[lax.rem(z - d + T, T)] = weights[d][...]
    packed = jnp.concatenate([r[...] for r in rows], axis=0)
    low = jnp.zeros((X * CAP, RANK), jnp.float32)
    for w in range(T):
        first = w * SLICE // 128 * 128
        low += dot(packed[:, first:first + PAD], held[w, :, :PAD], 1, 1)
    low = low.astype(jnp.bfloat16)
    for w in range(T):
        delta = dot(low, held[w, :, PAD:]).astype(jnp.bfloat16)
        for d in range(X):
            out[lax.rem(x - d + X, X), w] = delta[d * CAP:(d + 1) * CAP, :]


def adapt(rows, weights):
    return pl.pallas_call(
        adapt_kernel,
        in_specs=[pl.BlockSpec(memory_space=pltpu.VMEM)] * (X + T),
        out_specs=pl.BlockSpec(memory_space=pltpu.VMEM),
        out_shape=jax.ShapeDtypeStruct((X, T, CAP, UP), jnp.bfloat16),
        scratch_shapes=[
            pltpu.VMEM((T, RANK, PAD + UP), jnp.bfloat16),
            pltpu.VMEM((X * CAP, RANK), jnp.float32),
        ],
        cost_estimate=pl.CostEstimate(
            flops=2 * 128 * RANK * (WIDTH + 2048), bytes_accessed=3_000_000, transcendentals=0
        ),
        name="adapt",
    )(*rows, *weights)


def attend_kernel(delta_ref, q_ref, kv0, kv1, kv2, cos_ref, sin_ref, gain_ref, lower_ref, column_ref,
                  out_ref):
    half = ROWS // 2
    slot = lax.broadcasted_iota(jnp.int32, (ROWS, HEAD), 1)
    column = column_ref[...]
    chosen = jnp.concatenate(
        [(column == slot + c * HEAD).astype(jnp.float32).astype(jnp.bfloat16)
         for c in range(SLOTS // HEAD)], axis=1)
    query = q_ref[...] + dot(chosen, delta_ref[...])
    turned = [
        (turn(unit(query[:, h * HEAD:(h + 1) * HEAD], gain_ref[...]), cos_ref[...], sin_ref[...])
         ).astype(jnp.bfloat16)
        for h in range(2)
    ]
    for tile in range(2):
        here = slice(tile * half, (tile + 1) * half)
        q = jnp.concatenate([turned[0][here], turned[1][here]], axis=0)
        pieces = ((kv0, tile * half, ROWS), (kv1, 0, ROWS), (kv2, 0, (tile + 1) * half))
        low = lower_ref[here, :1]
        high = WINDOW + tile * half + lax.broadcasted_iota(jnp.int32, (half, 1), 0)
        scores = []
        for n, (ref, a, b) in enumerate(pieces):
            s = dot(q, ref[a:b, :HEAD], 1, 1) * QUERY_SCALE
            at = n * ROWS + a + lax.broadcasted_iota(jnp.int32, (half, b - a), 1)
            allowed = at >= low
            if n == 2:
                allowed = allowed & (at <= high)
            scores.append(jnp.where(jnp.concatenate([allowed, allowed], axis=0), s, -1e30))
        peak = functools.reduce(
            jnp.maximum, [jnp.max(s, axis=-1, keepdims=True) for s in scores])
        weights = [jnp.exp(s - peak) for s in scores]
        total = sum(jnp.sum(w, axis=-1, keepdims=True) for w in weights)
        mixed = sum(
            dot(w.astype(jnp.bfloat16), ref[a:b, HEAD:])
            for w, (ref, a, b) in zip(weights, pieces))
        mixed = (mixed / total).astype(jnp.bfloat16)
        out_ref[here, :HEAD] = mixed[:half]
        out_ref[here, HEAD:] = mixed[half:]


def attend(*args):
    return pl.pallas_call(
        attend_kernel,
        in_specs=[pl.BlockSpec(memory_space=pltpu.VMEM)] * 10,
        out_specs=pl.BlockSpec(memory_space=pltpu.VMEM),
        out_shape=jax.ShapeDtypeStruct((ROWS, 2 * HEAD), jnp.bfloat16),
        cost_estimate=pl.CostEstimate(
            flops=4 * 1024 * 1280 * HEAD, bytes_accessed=4_000_000, transcendentals=1024 * 1280
        ),
        name="attend",
    )(*args)


def body(
    tokens, query_weight, key_weight, value_weight, query_norm_gain, key_norm_gain,
    adapter_down_weight, adapter_up_weight, token_adapter_index, packed_prompt_length,
):
    x, z, t = lax.axis_index("x"), lax.axis_index("z"), lax.axis_index("tp")
    down = jnp.swapaxes(adapter_down_weight[0], 0, 1)
    carried = jnp.concatenate([jnp.zeros((RANK, PAD), jnp.bfloat16), adapter_up_weight[0]], axis=1)
    carried = lax.dynamic_update_slice(carried, down, (0, lax.rem(t * SLICE, 128)))
    weights = [
        lax.ppermute(carried, ("z", "tp"),
                     [(a * T + w, (w + d) % Z * T + a) for a in range(Z) for w in range(T)])
        for d in range(T)
    ]
    *rows, target = pack(token_adapter_index.reshape(1, ROWS), tokens)
    rows = [rows[0]] + [
        lax.ppermute(rows[d], "x", [(i, (i + d) % X) for i in range(X)]) for d in range(1, X)
    ]
    place = ((x * Z + z) * ROWS + jnp.arange(ROWS, dtype=jnp.int32)).astype(jnp.float32)
    half = HEAD // 2
    freq = jnp.exp(
        -(2.0 * jnp.arange(half, dtype=jnp.float32) / HEAD) * jnp.log(jnp.float32(10000.0)))
    angle = place[:, None] * freq[None, :]
    cosine, sine = jnp.cos(angle), jnp.sin(angle)
    cosine = jnp.concatenate([cosine, cosine], axis=1)
    sine = jnp.concatenate([-sine, sine], axis=1)
    query, kv, lower, column = project(
        packed_prompt_length, tokens, query_weight, key_weight, value_weight,
        cosine, sine, key_norm_gain.reshape(1, HEAD), target)
    earlier = [
        lax.ppermute(kv, ("x", "z"), [(i, i + d) for i in range(X * Z - d)])
        for d in (2, 1)
    ]
    delta = adapt(rows, weights)
    delta = lax.all_to_all(delta.reshape(X * T, CAP, UP), ("x", "tp"), 0, 0)
    return attend(delta.reshape(SLOTS, UP), query, *earlier, kv, cosine, sine,
                  query_norm_gain.reshape(1, HEAD), lower, column)


def solution(mesh):
    mesh = Mesh(mesh.devices.reshape(X, Z, T), ("x", "z", "tp"))
    seq = ("x", "z")
    in_specs = (
        P(seq, None), P(None, "tp"), P(None, "tp"), P(None, "tp"), P(), P(),
        P(seq, "tp", None), P(seq, None, "tp"), P(seq, None), P(),
    )
    return jax.shard_map(
        body, mesh=mesh, in_specs=in_specs, out_specs=P(seq, "tp"), check_vma=False)
```

```python
import functools
import jax
import jax.numpy as jnp
from jax import lax
from jax.experimental import pallas as pl
from jax.experimental.pallas import tpu as pltpu
from jax.sharding import Mesh, PartitionSpec as P

WINDOW = 1024
QUERY_SCALE = 0.07715167498104596
X, Z, T = 4, 8, 8
ROWS, WIDTH, HEAD, RANK, CAP = 512, 5376, 128, 64, 32
SLICE = WIDTH // T
PAD = 768
STEP = 768
STEPS = WIDTH // STEP
UP = 256
SLOTS = X * T * CAP
NEAR = (0, 1, Z - 1, 2)


def dot(a, b, ca=1, cb=0):
    return lax.dot_general(a, b, (((ca,), (cb,)), ((), ())), preferred_element_type=jnp.float32)


def pack_kernel(idx_ref, x_ref, out0, out1, out2, out3, target_ref, pick, held, sems):
    copies = [
        pltpu.make_async_copy(x_ref.at[:, pl.ds(j * STEP, STEP)], held.at[j], sems.at[j])
        for j in range(STEPS)
    ]
    for copy in copies:
        copy.start()
    x, t = lax.axis_index("x"), lax.axis_index("tp")
    idx = idx_ref[...]
    named = lax.broadcasted_iota(jnp.int32, (X * T, ROWS), 0) == idx
    earlier = lax.broadcasted_iota(jnp.int32, (ROWS, ROWS), 0) < lax.broadcasted_iota(
        jnp.int32, (ROWS, ROWS), 1
    )
    before = dot(named.astype(jnp.float32).astype(jnp.bfloat16),
                 earlier.astype(jnp.float32).astype(jnp.bfloat16))
    rank = jnp.sum(jnp.where(named, before, 0.0), axis=0, keepdims=True).astype(jnp.int32)
    target = idx * CAP + rank
    target_ref[...] = target
    slot = lax.broadcasted_iota(jnp.int32, (CAP, ROWS), 0)
    for d in range(X):
        adapter = lax.rem(x + d, X) * T + t
        pick[d * CAP:(d + 1) * CAP, :] = (
            (slot + adapter * CAP == target).astype(jnp.float32).astype(jnp.bfloat16)
        )
    for j in range(STEPS):
        copies[j].wait()
        packed = dot(pick[...], held[j]).astype(jnp.bfloat16)
        for d, out in enumerate((out0, out1, out2, out3)):
            out[:, j * STEP:(j + 1) * STEP] = packed[d * CAP:(d + 1) * CAP, :]


def pack(idx, tokens):
    row = jax.ShapeDtypeStruct((CAP, WIDTH), jnp.bfloat16)
    return pl.pallas_call(
        pack_kernel,
        in_specs=[pl.BlockSpec(memory_space=pltpu.VMEM), pl.BlockSpec(memory_space=pl.ANY)],
        out_specs=[pl.BlockSpec(memory_space=pltpu.VMEM)] * (X + 1),
        out_shape=[row] * X + [jax.ShapeDtypeStruct((1, ROWS), jnp.int32)],
        scratch_shapes=[
            pltpu.VMEM((X * CAP, ROWS), jnp.bfloat16),
            pltpu.VMEM((STEPS, ROWS, STEP), jnp.bfloat16),
            pltpu.SemaphoreType.DMA((STEPS,)),
        ],
        cost_estimate=pl.CostEstimate(
            flops=2 * X * CAP * ROWS * WIDTH, bytes_accessed=7_000_000, transcendentals=0
        ),
        name="pack",
    )(idx, tokens)


def unit(field, gain):
    return field / jnp.sqrt(jnp.mean(field * field, axis=-1, keepdims=True) + 1e-06) * gain


def turn(field, cosine, sine):
    return field * cosine + pltpu.roll(field, HEAD // 2, 1) * sine


def project_kernel(
    lens_ref, x_ref, wq_ref, wk_ref, wv_ref, cos_ref, sin_ref, gain_ref, target_ref,
    q_ref, kv_ref, lower_ref, column_ref, x_held, q_held, kv_held, acc, sems,
):
    copies = []
    for j in range(STEPS):
        part = pl.ds(j * STEP, STEP)
        pairs = (
            (x_ref.at[:, part], x_held.at[j]),
            (wk_ref.at[part, :], kv_held.at[j, :, pl.ds(0, HEAD)]),
            (wv_ref.at[part, :], kv_held.at[j, :, pl.ds(HEAD, HEAD)]),
            (wq_ref.at[part, :], q_held.at[j]),
        )
        copies.append([
            pltpu.make_async_copy(source, target, sems.at[j, n])
            for n, (source, target) in enumerate(pairs)
        ])
    for group in copies:
        for copy in group:
            copy.start()
    begin = (lax.axis_index("x") * Z + lax.axis_index("z")) * ROWS
    place = begin + lax.broadcasted_iota(jnp.int32, (ROWS, HEAD), 0)
    start = jnp.zeros((ROWS, HEAD), jnp.int32)
    at = jnp.int32(0)
    for i in range(lens_ref.shape[0]):
        start = jnp.where(place >= at, at, start)
        at = at + lens_ref[i]
    lower_ref[...] = jnp.maximum(start, place - (WINDOW - 1)) - (begin - WINDOW)
    wide = jnp.broadcast_to(target_ref[...].astype(jnp.float32), (HEAD, ROWS))
    column_ref[...] = jnp.transpose(wide).astype(jnp.int32)
    for j in range(STEPS):
        for copy in copies[j]:
            copy.wait()
        q = dot(x_held[j], q_held[j])
        kv = dot(x_held[j], kv_held[j])
        if j == 0:
            q_ref[...] = q
            acc[...] = kv
        else:
            q_ref[...] += q
            acc[...] += kv
    key = turn(unit(acc[:, :HEAD], gain_ref[...]), cos_ref[...], sin_ref[...])
    kv_ref[:, :HEAD] = key.astype(jnp.bfloat16)
    kv_ref[:, HEAD:] = acc[:, HEAD:].astype(jnp.bfloat16)


def project(lens, tokens, wq, wk, wv, cosine, sine, gain, target):
    near, far = pl.BlockSpec(memory_space=pltpu.VMEM), pl.BlockSpec(memory_space=pl.ANY)
    return pl.pallas_call(
        project_kernel,
        in_specs=[pl.BlockSpec(memory_space=pltpu.SMEM)] + [far] * 4 + [near] * 4,
        out_specs=[near] * 4,
        out_shape=[
            jax.ShapeDtypeStruct((ROWS, 2 * HEAD), jnp.float32),
            jax.ShapeDtypeStruct((ROWS, 2 * HEAD), jnp.bfloat16),
            jax.ShapeDtypeStruct((ROWS, HEAD), jnp.int32),
            jax.ShapeDtypeStruct((ROWS, HEAD), jnp.int32),
        ],
        scratch_shapes=[
            pltpu.VMEM((STEPS, ROWS, STEP), jnp.bfloat16),
            pltpu.VMEM((STEPS, STEP, 2 * HEAD), jnp.bfloat16),
            pltpu.VMEM((STEPS, STEP, 2 * HEAD), jnp.bfloat16),
            pltpu.VMEM((ROWS, 2 * HEAD), jnp.float32),
            pltpu.SemaphoreType.DMA((STEPS, 4)),
        ],
        cost_estimate=pl.CostEstimate(
            flops=2 * ROWS * WIDTH * 512, bytes_accessed=12_500_000, transcendentals=0
        ),
        name="project",
    )(lens, tokens, wq, wk, wv, cosine, sine, gain, target)


def adapt_kernel(*refs):
    rows, weights, out, held = refs[:X], refs[X:X + 4], refs[X + 4], refs[X + 5]
    x, z = lax.axis_index("x"), lax.axis_index("z")
    for d in range(4):
        for n in range(2):
            held[lax.rem(z + NEAR[d] + 4 * n, T)] = weights[d][n * RANK:(n + 1) * RANK, :]
    packed = jnp.concatenate([r[...] for r in rows], axis=0)
    low = jnp.zeros((X * CAP, RANK), jnp.float32)
    for w in range(T):
        first = w * SLICE // 128 * 128
        low += dot(packed[:, first:first + PAD], held[w, :, :PAD], 1, 1)
    low = low.astype(jnp.bfloat16)
    for w in range(T):
        delta = dot(low, held[w, :, PAD:]).astype(jnp.bfloat16)
        for d in range(X):
            out[lax.rem(x - d + X, X), w] = delta[d * CAP:(d + 1) * CAP, :]


def adapt(rows, weights):
    return pl.pallas_call(
        adapt_kernel,
        in_specs=[pl.BlockSpec(memory_space=pltpu.VMEM)] * (X + 4),
        out_specs=pl.BlockSpec(memory_space=pltpu.VMEM),
        out_shape=jax.ShapeDtypeStruct((X, T, CAP, UP), jnp.bfloat16),
        scratch_shapes=[
            pltpu.VMEM((T, RANK, PAD + UP), jnp.bfloat16),
        ],
        cost_estimate=pl.CostEstimate(
            flops=2 * 128 * RANK * (WIDTH + 2048), bytes_accessed=3_000_000, transcendentals=0
        ),
        name="adapt",
    )(*rows, *weights)


def attend_kernel(delta_ref, q_ref, kv0, kv1, kv2, cos_ref, sin_ref, gain_ref, lower_ref, column_ref,
                  out_ref):
    half = ROWS // 2
    slot = lax.broadcasted_iota(jnp.int32, (ROWS, HEAD), 1)
    column = column_ref[...]
    chosen = jnp.concatenate(
        [(column == slot + c * HEAD).astype(jnp.float32).astype(jnp.bfloat16)
         for c in range(SLOTS // HEAD)], axis=1)
    query = q_ref[...] + dot(chosen, delta_ref[...])
    turned = [
        (turn(unit(query[:, h * HEAD:(h + 1) * HEAD], gain_ref[...]), cos_ref[...], sin_ref[...])
         ).astype(jnp.bfloat16)
        for h in range(2)
    ]
    for tile in range(2):
        here = slice(tile * half, (tile + 1) * half)
        q = jnp.concatenate([turned[0][here], turned[1][here]], axis=0)
        pieces = ((kv0, tile * half, ROWS), (kv1, 0, ROWS), (kv2, 0, (tile + 1) * half))
        low = lower_ref[here, :1]
        high = WINDOW + tile * half + lax.broadcasted_iota(jnp.int32, (half, 1), 0)
        scores = []
        for n, (ref, a, b) in enumerate(pieces):
            s = dot(q, ref[a:b, :HEAD], 1, 1) * QUERY_SCALE
            at = n * ROWS + a + lax.broadcasted_iota(jnp.int32, (half, b - a), 1)
            allowed = at >= low
            if n == 2:
                allowed = allowed & (at <= high)
            scores.append(jnp.where(jnp.concatenate([allowed, allowed], axis=0), s, -1e30))
        peak = functools.reduce(
            jnp.maximum, [jnp.max(s, axis=-1, keepdims=True) for s in scores])
        weights = [jnp.exp(s - peak) for s in scores]
        total = sum(jnp.sum(w, axis=-1, keepdims=True) for w in weights)
        mixed = sum(
            dot(w.astype(jnp.bfloat16), ref[a:b, HEAD:])
            for w, (ref, a, b) in zip(weights, pieces))
        mixed = (mixed / total).astype(jnp.bfloat16)
        out_ref[here, :HEAD] = mixed[:half]
        out_ref[here, HEAD:] = mixed[half:]


def attend(*args):
    return pl.pallas_call(
        attend_kernel,
        in_specs=[pl.BlockSpec(memory_space=pltpu.VMEM)] * 10,
        out_specs=pl.BlockSpec(memory_space=pltpu.VMEM),
        out_shape=jax.ShapeDtypeStruct((ROWS, 2 * HEAD), jnp.bfloat16),
        cost_estimate=pl.CostEstimate(
            flops=4 * 1024 * 1280 * HEAD, bytes_accessed=4_000_000, transcendentals=1024 * 1280
        ),
        name="attend",
    )(*args)


def layer(
    tokens, query_weight, key_weight, value_weight, query_norm_gain, key_norm_gain,
    adapter_down_weight, adapter_up_weight, token_adapter_index, packed_prompt_length,
):
    x, z, t = lax.axis_index("x"), lax.axis_index("z"), lax.axis_index("tp")
    down = jnp.swapaxes(adapter_down_weight[0], 0, 1)
    shift = lax.rem(t * SLICE, 128)
    down = functools.reduce(
        lambda other, at: jnp.where(
            shift == at, jnp.pad(down, ((0, 0), (at, PAD - SLICE - at))), other),
        (32, 64, 96), jnp.pad(down, ((0, 0), (0, PAD - SLICE))))
    carried = jnp.concatenate([down, adapter_up_weight[0]], axis=1)
    weights = [
        lax.ppermute(
            carried, ("z", "tp"),
            [(a * T + w, (w + d) % Z * T + a) for a in range(Z) for w in range(T)])
        for d in (0, 4)
    ]
    weights = jnp.concatenate(weights, axis=0)
    weights = [weights] + [
        lax.ppermute(
            weights, "z", [((i + d) % Z, i) for i in range(Z)])
        for d in NEAR[1:]
    ]
    *rows, target = pack(token_adapter_index.reshape(1, ROWS), tokens)
    rows = [rows[0]] + [
        lax.ppermute(
            rows[d], "x", [(i, (i + d) % X) for i in range(X)])
        for d in range(1, X)
    ]
    place = ((x * Z + z) * ROWS + jnp.arange(ROWS, dtype=jnp.int32)).astype(jnp.float32)
    half = HEAD // 2
    freq = jnp.exp(
        -(2.0 * jnp.arange(half, dtype=jnp.float32) / HEAD) * jnp.log(jnp.float32(10000.0)))
    angle = place[:, None] * freq[None, :]
    cosine, sine = jnp.cos(angle), jnp.sin(angle)
    cosine = jnp.concatenate([cosine, cosine], axis=1)
    sine = jnp.concatenate([-sine, sine], axis=1)
    query, kv, lower, column = project(
        packed_prompt_length, tokens, query_weight, key_weight, value_weight,
        cosine, sine, key_norm_gain.reshape(1, HEAD), target)
    onward = [(i, i + 1) for i in range(X * Z - 1)]
    kv1 = lax.ppermute(kv, ("x", "z"), onward)
    kv0 = lax.ppermute(kv1, ("x", "z"), onward)
    delta = adapt(rows, weights)
    delta = lax.all_to_all(
        delta.reshape(X * T, CAP, UP), ("x", "tp"), 0, 0)
    return attend(
        delta.reshape(SLOTS, UP), query, kv0, kv1, kv, cosine, sine,
        query_norm_gain.reshape(1, HEAD), lower, column)


def solution(mesh):
    mesh = Mesh(mesh.devices.reshape(X, Z, T), ("x", "z", "tp"))
    seq = ("x", "z")
    in_specs = (
        P(seq, None), P(None, "tp"), P(None, "tp"), P(None, "tp"), P(), P(),
        P(seq, "tp", None), P(seq, None, "tp"), P(seq, None), P(),
    )
    return jax.shard_map(
        layer, mesh=mesh, in_specs=in_specs, out_specs=P(seq, "tp"), check_vma=False)
```

```python
import functools
import jax
import jax.numpy as jnp
from jax import lax
from jax.experimental import pallas as pl
from jax.experimental.pallas import tpu as pltpu
from jax.sharding import Mesh, PartitionSpec as P

WINDOW = 1024
QUERY_SCALE = 0.07715167498104596
LOG2E = 1.4426950408889634
X, Z, T = 4, 8, 8
ROWS, WIDTH, HEAD, RANK, CAP = 512, 5376, 128, 64, 32
SLICE = WIDTH // T
PAD = 768
STEP = 768
STEPS = WIDTH // STEP
UP = 256
SLOTS = X * T * CAP
NEAR = (0, 1, Z - 1, 2)


def dot(a, b, ca=1, cb=0):
    return lax.dot_general(a, b, (((ca,), (cb,)), ((), ())), preferred_element_type=jnp.float32)


def pack_kernel(idx_ref, x_ref, out0, out1, out2, out3, target_ref, pick, held, sems):
    copies = [
        pltpu.make_async_copy(x_ref.at[:, pl.ds(j * STEP, STEP)], held.at[j], sems.at[j])
        for j in range(STEPS)
    ]
    for copy in copies:
        copy.start()
    x, t = lax.axis_index("x"), lax.axis_index("tp")
    idx = idx_ref[...]
    named = lax.broadcasted_iota(jnp.int32, (X * T, ROWS), 0) == idx
    earlier = lax.broadcasted_iota(jnp.int32, (ROWS, ROWS), 0) < lax.broadcasted_iota(
        jnp.int32, (ROWS, ROWS), 1
    )
    before = dot(named.astype(jnp.float32).astype(jnp.bfloat16),
                 earlier.astype(jnp.float32).astype(jnp.bfloat16))
    rank = jnp.sum(jnp.where(named, before, 0.0), axis=0, keepdims=True).astype(jnp.int32)
    target = idx * CAP + rank
    target_ref[...] = target
    slot = lax.broadcasted_iota(jnp.int32, (CAP, ROWS), 0)
    for d in range(X):
        adapter = lax.rem(x + d, X) * T + t
        pick[d * CAP:(d + 1) * CAP, :] = (
            (slot + adapter * CAP == target).astype(jnp.float32).astype(jnp.bfloat16)
        )
    for j in range(STEPS):
        copies[j].wait()
        packed = dot(pick[...], held[j]).astype(jnp.bfloat16)
        for d, out in enumerate((out0, out1, out2, out3)):
            out[:, j * STEP:(j + 1) * STEP] = packed[d * CAP:(d + 1) * CAP, :]


def pack(idx, tokens):
    row = jax.ShapeDtypeStruct((CAP, WIDTH), jnp.bfloat16)
    return pl.pallas_call(
        pack_kernel,
        in_specs=[pl.BlockSpec(memory_space=pltpu.VMEM), pl.BlockSpec(memory_space=pl.ANY)],
        out_specs=[pl.BlockSpec(memory_space=pltpu.VMEM)] * (X + 1),
        out_shape=[row] * X + [jax.ShapeDtypeStruct((1, ROWS), jnp.int32)],
        scratch_shapes=[
            pltpu.VMEM((X * CAP, ROWS), jnp.bfloat16),
            pltpu.VMEM((STEPS, ROWS, STEP), jnp.bfloat16),
            pltpu.SemaphoreType.DMA((STEPS,)),
        ],
        cost_estimate=pl.CostEstimate(
            flops=2 * X * CAP * ROWS * WIDTH, bytes_accessed=7_000_000, transcendentals=0
        ),
        name="pack",
    )(idx, tokens)


def unit(field, gain):
    return field / jnp.sqrt(jnp.mean(field * field, axis=-1, keepdims=True) + 1e-06) * gain


def turn(field, cosine, sine):
    return field * cosine + pltpu.roll(field, HEAD // 2, 1) * sine


def project_kernel(
    lens_ref, x_ref, wq_ref, wk_ref, wv_ref, gain_ref, target_ref,
    q_ref, kv_ref, lower_ref, column_ref, cos_ref, sin_ref, x_held, q_held, kv_held, acc, sems,
):
    copies = []
    for j in range(STEPS):
        part = pl.ds(j * STEP, STEP)
        pairs = (
            (x_ref.at[:, part], x_held.at[j]),
            (wk_ref.at[part, :], kv_held.at[j, :, pl.ds(0, HEAD)]),
            (wv_ref.at[part, :], kv_held.at[j, :, pl.ds(HEAD, HEAD)]),
            (wq_ref.at[part, :], q_held.at[j]),
        )
        copies.append([
            pltpu.make_async_copy(source, target, sems.at[j, n])
            for n, (source, target) in enumerate(pairs)
        ])
    for group in copies:
        for copy in group:
            copy.start()
    begin = (lax.axis_index("x") * Z + lax.axis_index("z")) * ROWS
    place = begin + lax.broadcasted_iota(jnp.int32, (ROWS, HEAD), 0)
    start = jnp.zeros((ROWS, HEAD), jnp.int32)
    at = jnp.int32(0)
    for i in range(lens_ref.shape[0]):
        start = jnp.where(place >= at, at, start)
        at = at + lens_ref[i]
    lower_ref[...] = jnp.maximum(start, place - (WINDOW - 1)) - (begin - WINDOW)
    wide = jnp.broadcast_to(target_ref[...].astype(jnp.float32), (HEAD, ROWS))
    column_ref[...] = jnp.transpose(wide).astype(jnp.int32)
    lane = lax.broadcasted_iota(jnp.int32, (ROWS, HEAD), 1)
    pair = jnp.bitwise_and(lane, HEAD // 2 - 1).astype(jnp.float32)
    angle = place.astype(jnp.float32) * jnp.exp(-(2.0 * pair / HEAD) * jnp.log(jnp.float32(10000.0)))
    cos_ref[...] = jnp.cos(angle)
    sine = jnp.sin(angle)
    sin_ref[...] = jnp.where(lane < HEAD // 2, -sine, sine)
    for j in range(STEPS):
        for copy in copies[j]:
            copy.wait()
        q = dot(x_held[j], q_held[j])
        kv = dot(x_held[j], kv_held[j])
        if j == 0:
            q_ref[...] = q
            acc[...] = kv
        else:
            q_ref[...] += q
            acc[...] += kv
    key = turn(unit(acc[:, :HEAD], gain_ref[...]), cos_ref[...], sin_ref[...])
    kv_ref[:, :HEAD] = key.astype(jnp.bfloat16)
    kv_ref[:, HEAD:] = acc[:, HEAD:].astype(jnp.bfloat16)


def project(lens, tokens, wq, wk, wv, gain, target):
    near, far = pl.BlockSpec(memory_space=pltpu.VMEM), pl.BlockSpec(memory_space=pl.ANY)
    return pl.pallas_call(
        project_kernel,
        in_specs=[pl.BlockSpec(memory_space=pltpu.SMEM)] + [far] * 4 + [near] * 2,
        out_specs=[near] * 6,
        out_shape=[
            jax.ShapeDtypeStruct((ROWS, 2 * HEAD), jnp.float32),
            jax.ShapeDtypeStruct((ROWS, 2 * HEAD), jnp.bfloat16),
            jax.ShapeDtypeStruct((ROWS, HEAD), jnp.int32),
            jax.ShapeDtypeStruct((ROWS, HEAD), jnp.int32),
            jax.ShapeDtypeStruct((ROWS, HEAD), jnp.float32),
            jax.ShapeDtypeStruct((ROWS, HEAD), jnp.float32),
        ],
        scratch_shapes=[
            pltpu.VMEM((STEPS, ROWS, STEP), jnp.bfloat16),
            pltpu.VMEM((STEPS, STEP, 2 * HEAD), jnp.bfloat16),
            pltpu.VMEM((STEPS, STEP, 2 * HEAD), jnp.bfloat16),
            pltpu.VMEM((ROWS, 2 * HEAD), jnp.float32),
            pltpu.SemaphoreType.DMA((STEPS, 4)),
        ],
        cost_estimate=pl.CostEstimate(
            flops=2 * ROWS * WIDTH * 512, bytes_accessed=12_500_000, transcendentals=0
        ),
        name="project",
    )(lens, tokens, wq, wk, wv, gain, target)


def adapt_kernel(*refs):
    rows, weights, out = refs[:X], refs[X:X + 4], refs[X + 4]
    packed, held, sems = refs[X + 5:]
    x, z = lax.axis_index("x"), lax.axis_index("z")
    copies = [
        pltpu.make_async_copy(
            weights[d].at[pl.ds(n * RANK, RANK), :],
            held.at[lax.rem(z + NEAR[d] + 4 * n, T)], sems.at[X + 2 * d + n])
        for d in range(4) for n in range(2)
    ] + [
        pltpu.make_async_copy(rows[d], packed.at[pl.ds(d * CAP, CAP), :], sems.at[d])
        for d in range(X)
    ]
    for copy in copies:
        copy.start()
    for copy in copies:
        copy.wait()
    low = jnp.zeros((X * CAP, RANK), jnp.float32)
    for w in range(T):
        first = w * SLICE // 128 * 128
        low += dot(packed[:, first:first + PAD], held[w, :, :PAD], 1, 1)
    low = low.astype(jnp.bfloat16)
    for w in range(T):
        delta = dot(low, held[w, :, PAD:]).astype(jnp.bfloat16)
        for d in range(X):
            out[lax.rem(x - d + X, X), w] = delta[d * CAP:(d + 1) * CAP, :]


def adapt(rows, weights):
    return pl.pallas_call(
        adapt_kernel,
        in_specs=[pl.BlockSpec(memory_space=pl.ANY)] * (X + 4),
        out_specs=pl.BlockSpec(memory_space=pltpu.VMEM),
        out_shape=jax.ShapeDtypeStruct((X, T, CAP, UP), jnp.bfloat16),
        scratch_shapes=[
            pltpu.VMEM((X * CAP, WIDTH), jnp.bfloat16),
            pltpu.VMEM((T, RANK, PAD + UP), jnp.bfloat16),
            pltpu.SemaphoreType.DMA((X + T,)),
        ],
        compiler_params=pltpu.CompilerParams(vmem_limit_bytes=12 << 20),
        cost_estimate=pl.CostEstimate(
            flops=2 * 128 * RANK * (WIDTH + 2048), bytes_accessed=3_000_000, transcendentals=0
        ),
        name="adapt",
    )(*rows, *weights)


def attend_kernel(delta_hbm, column_hbm, q_hbm, cos_hbm, sin_hbm, lower_hbm, kv0_hbm, kv1_hbm, kv2_hbm,
                  gain_ref, out_ref, delta_ref, column_ref, q_ref, cos_ref, sin_ref, lower_ref,
                  kv_ref, sems):
    half = ROWS // 2
    pairs = [
        (column_hbm, column_ref), (delta_hbm, delta_ref), (q_hbm, q_ref), (cos_hbm, cos_ref),
        (sin_hbm, sin_ref), (lower_hbm, lower_ref),
    ] + [
        (source.at[:, pl.ds(n * HEAD, HEAD)], kv_ref.at[pl.ds(b * ROWS, ROWS), pl.ds(n * HEAD, HEAD)])
        for b, source in enumerate((kv0_hbm, kv1_hbm, kv2_hbm)) for n in range(2)
    ]
    copies = [
        pltpu.make_async_copy(source, target, sems.at[n])
        for n, (source, target) in enumerate(pairs)
    ]
    for copy in copies:
        copy.start()
    kv_ref[:, 2 * HEAD:] = jnp.ones((3 * ROWS, HEAD), jnp.bfloat16)
    slot = lax.broadcasted_iota(jnp.int32, (ROWS, HEAD), 1)
    copies[0].wait()
    column = column_ref[...]
    chosen = jnp.concatenate(
        [(column == slot + c * HEAD).astype(jnp.float32).astype(jnp.bfloat16)
         for c in range(SLOTS // HEAD)], axis=1)
    copies[1].wait()
    delta = dot(chosen, delta_ref[...])
    for copy in copies[2:5]:
        copy.wait()
    query = q_ref[...] + delta
    gain = gain_ref[...] * (QUERY_SCALE * LOG2E)
    turned = [
        turn(unit(query[:, h * HEAD:(h + 1) * HEAD], gain), cos_ref[...], sin_ref[...]
             ).astype(jnp.bfloat16)
        for h in range(2)
    ]
    for copy in copies[5:]:
        copy.wait()
    for tile in range(2):
        here = slice(tile * half, (tile + 1) * half)
        first, past = tile * half, tile * half + WINDOW + half
        q = jnp.concatenate([turned[0][here], turned[1][here]], axis=0)
        s = dot(q, kv_ref[first:past, :HEAD], 1, 1)
        low = lower_ref[here, :1] - first
        at = lax.broadcasted_iota(jnp.int32, (half, WINDOW + half), 1)
        high = WINDOW + lax.broadcasted_iota(jnp.int32, (half, 1), 0)
        allowed = (at >= low) & (at <= high)
        s = jnp.where(jnp.concatenate([allowed, allowed], axis=0), s, -1e30)
        peak = jnp.max(s, axis=-1, keepdims=True)
        weights = jnp.exp2(s - peak).astype(jnp.bfloat16)
        mixed = dot(weights, kv_ref[first:past, HEAD:])
        mixed = (mixed[:, :HEAD] / mixed[:, HEAD:]).astype(jnp.bfloat16)
        out_ref[here, :HEAD] = mixed[:half]
        out_ref[here, HEAD:] = mixed[half:]


def attend(*args):
    near, far = pl.BlockSpec(memory_space=pltpu.VMEM), pl.BlockSpec(memory_space=pl.ANY)
    return pl.pallas_call(
        attend_kernel,
        in_specs=[far] * 9 + [near],
        out_specs=near,
        out_shape=jax.ShapeDtypeStruct((ROWS, 2 * HEAD), jnp.bfloat16),
        scratch_shapes=[
            pltpu.VMEM((SLOTS, UP), jnp.bfloat16),
            pltpu.VMEM((ROWS, HEAD), jnp.int32),
            pltpu.VMEM((ROWS, 2 * HEAD), jnp.float32),
            pltpu.VMEM((ROWS, HEAD), jnp.float32),
            pltpu.VMEM((ROWS, HEAD), jnp.float32),
            pltpu.VMEM((ROWS, HEAD), jnp.int32),
            pltpu.VMEM((3 * ROWS, 3 * HEAD), jnp.bfloat16),
            pltpu.SemaphoreType.DMA((12,)),
        ],
        compiler_params=pltpu.CompilerParams(vmem_limit_bytes=24 << 20),
        cost_estimate=pl.CostEstimate(
            flops=4 * 1024 * 1280 * HEAD, bytes_accessed=4_000_000, transcendentals=1024 * 1280
        ),
        name="attend",
    )(*args)


def layer(
    tokens, query_weight, key_weight, value_weight, query_norm_gain, key_norm_gain,
    adapter_down_weight, adapter_up_weight, token_adapter_index, packed_prompt_length,
):
    t = lax.axis_index("tp")
    down = jnp.swapaxes(adapter_down_weight[0], 0, 1)
    shift = lax.rem(t * SLICE, 128)
    carried = functools.reduce(
        lambda other, at: jnp.where(
            shift == at, jnp.pad(down, ((0, 0), (at, PAD + UP - SLICE - at))), other),
        (32, 64, 96), jnp.pad(down, ((0, 0), (0, PAD + UP - SLICE))))
    carried = jnp.where(
        jnp.arange(PAD + UP)[None, :] < PAD, carried,
        jnp.pad(adapter_up_weight[0], ((0, 0), (PAD, 0))))
    weights = [
        lax.ppermute(
            carried, ("z", "tp"),
            [(a * T + w, (w + d) % Z * T + a) for a in range(Z) for w in range(T)])
        for d in (0, 4)
    ]
    weights = jnp.concatenate(weights, axis=0)
    weights = [weights] + [
        lax.ppermute(
            weights, "z", [((i + d) % Z, i) for i in range(Z)])
        for d in NEAR[1:]
    ]
    *rows, target = pack(token_adapter_index.reshape(1, ROWS), tokens)
    rows = [rows[0]] + [
        lax.ppermute(
            rows[d], "x", [(i, (i + d) % X) for i in range(X)])
        for d in range(1, X)
    ]
    query, kv, lower, column, cosine, sine = project(
        packed_prompt_length, tokens, query_weight, key_weight, value_weight,
        key_norm_gain.reshape(1, HEAD), target)
    kv1, kv0 = [
        lax.ppermute(
            kv, ("x", "z"), [(i, i + d) for i in range(X * Z - d)])
        for d in (1, 2)
    ]
    delta = adapt(rows, weights)
    delta = lax.all_to_all(
        delta.reshape(X * T, CAP, UP), ("x", "tp"), 0, 0)
    return attend(
        delta.reshape(SLOTS, UP), column, query, cosine, sine, lower,
        kv0, kv1, kv, query_norm_gain.reshape(1, HEAD))


def solution(mesh):
    mesh = Mesh(mesh.devices.reshape(X, Z, T), ("x", "z", "tp"))
    seq = ("x", "z")
    in_specs = (
        P(seq, None), P(None, "tp"), P(None, "tp"), P(None, "tp"), P(), P(),
        P(seq, "tp", None), P(seq, None, "tp"), P(seq, None), P(),
    )
    return jax.shard_map(
        layer, mesh=mesh, in_specs=in_specs, out_specs=P(seq, "tp"), check_vma=False)
```

```python
import functools
import jax
import jax.numpy as jnp
from jax import lax
from jax.experimental import pallas as pl
from jax.experimental.pallas import tpu as pltpu
from jax.sharding import Mesh, PartitionSpec as P

WINDOW = 1024
QUERY_SCALE = 0.07715167498104596
LOG2E = 1.4426950408889634
X, Z, T = 4, 8, 8
ROWS, WIDTH, HEAD, RANK, CAP = 512, 5376, 128, 64, 32
SLICE = WIDTH // T
PAD = 768
STEP = 768
STEPS = WIDTH // STEP
UP = 256
SLOTS = X * T * CAP
COS, SIN, AUX, SIDE = 2 * HEAD, 3 * HEAD, 4 * HEAD, 5 * HEAD
NEAR = (0, 1, Z - 1, 2, Z - 2)
SPLIT = (2, 2, 2, 1, 1)
PARTS = len(NEAR)


def dot(a, b, ca=1, cb=0):
    return lax.dot_general(a, b, (((ca,), (cb,)), ((), ())), preferred_element_type=jnp.float32)


def pack_kernel(idx_ref, x_ref, out0, out1, out2, out3, target_ref, pick, held, sems):
    copies = [
        pltpu.make_async_copy(x_ref.at[:, pl.ds(j * STEP, STEP)], held.at[j], sems.at[j])
        for j in range(STEPS)
    ]
    for copy in copies:
        copy.start()
    x, t = lax.axis_index("x"), lax.axis_index("tp")
    idx = idx_ref[...]
    named = lax.broadcasted_iota(jnp.int32, (X * T, ROWS), 0) == idx
    earlier = lax.broadcasted_iota(jnp.int32, (ROWS, ROWS), 0) < lax.broadcasted_iota(
        jnp.int32, (ROWS, ROWS), 1
    )
    before = dot(named.astype(jnp.float32).astype(jnp.bfloat16),
                 earlier.astype(jnp.float32).astype(jnp.bfloat16))
    rank = jnp.sum(jnp.where(named, before, 0.0), axis=0, keepdims=True).astype(jnp.int32)
    target = idx * CAP + rank
    target_ref[...] = target
    slot = lax.broadcasted_iota(jnp.int32, (CAP, ROWS), 0)
    for d in range(X):
        adapter = lax.rem(x + d, X) * T + t
        pick[d * CAP:(d + 1) * CAP, :] = (
            (slot + adapter * CAP == target).astype(jnp.float32).astype(jnp.bfloat16)
        )
    for j in range(STEPS):
        copies[j].wait()
        packed = dot(pick[...], held[j]).astype(jnp.bfloat16)
        for d, out in enumerate((out0, out1, out2, out3)):
            out[:, j * STEP:(j + 1) * STEP] = packed[d * CAP:(d + 1) * CAP, :]


def pack(idx, tokens):
    row = jax.ShapeDtypeStruct((CAP, WIDTH), jnp.bfloat16)
    return pl.pallas_call(
        pack_kernel,
        in_specs=[pl.BlockSpec(memory_space=pltpu.VMEM), pl.BlockSpec(memory_space=pltpu.HBM)],
        out_specs=[pl.BlockSpec(memory_space=pltpu.VMEM)] * (X + 1),
        out_shape=[row] * X + [jax.ShapeDtypeStruct((1, ROWS), jnp.int32)],
        scratch_shapes=[
            pltpu.VMEM((X * CAP, ROWS), jnp.bfloat16),
            pltpu.VMEM((STEPS, ROWS, STEP), jnp.bfloat16),
            pltpu.SemaphoreType.DMA((STEPS,)),
        ],
        cost_estimate=pl.CostEstimate(
            flops=2 * X * CAP * ROWS * WIDTH, bytes_accessed=7_000_000, transcendentals=0
        ),
        compiler_params=pltpu.CompilerParams(vmem_limit_bytes=12 << 20),
        name="pack",
    )(idx, tokens)


def unit(field, gain):
    return field / jnp.sqrt(jnp.mean(field * field, axis=-1, keepdims=True) + 1e-06) * gain


def turn(field, cosine, sine):
    return field * cosine + pltpu.roll(field, HEAD // 2, 1) * sine


def project_kernel(
    lens_ref, x_ref, wq_ref, wk_ref, wv_ref, gain_ref, target_ref,
    side_ref, kv_ref, x_held, q_held, kv_held, acc, sems,
):
    copies = []
    for j in range(STEPS):
        part = pl.ds(j * STEP, STEP)
        pairs = (
            (x_ref.at[:, part], x_held.at[j]),
            (wk_ref.at[part, :], kv_held.at[j, :, pl.ds(0, HEAD)]),
            (wv_ref.at[part, :], kv_held.at[j, :, pl.ds(HEAD, HEAD)]),
            (wq_ref.at[part, :], q_held.at[j]),
        )
        copies.append([
            pltpu.make_async_copy(source, target, sems.at[j, n])
            for n, (source, target) in enumerate(pairs)
        ])
    for group in copies:
        for copy in group:
            copy.start()
    begin = (lax.axis_index("x") * Z + lax.axis_index("z")) * ROWS
    place = begin + lax.broadcasted_iota(jnp.int32, (ROWS, HEAD), 0)
    start = jnp.zeros((ROWS, HEAD), jnp.int32)
    at = jnp.int32(0)
    for i in range(lens_ref.shape[0]):
        start = jnp.where(place >= at, at, start)
        at = at + lens_ref[i]
    lower = jnp.maximum(start, place - (WINDOW - 1)) - (begin - WINDOW)
    wide = jnp.broadcast_to(target_ref[...].astype(jnp.float32), (HEAD, ROWS))
    lane = lax.broadcasted_iota(jnp.int32, (ROWS, HEAD), 1)
    side_ref[:, AUX:] = jnp.where(lane < HEAD // 2, lower.astype(jnp.float32), jnp.transpose(wide))
    pair = jnp.bitwise_and(lane, HEAD // 2 - 1).astype(jnp.float32)
    angle = place.astype(jnp.float32) * jnp.exp(-(2.0 * pair / HEAD) * jnp.log(jnp.float32(10000.0)))
    cosine = jnp.cos(angle)
    sine = jnp.sin(angle)
    sine = jnp.where(lane < HEAD // 2, -sine, sine)
    side_ref[:, COS:SIN] = cosine
    side_ref[:, SIN:AUX] = sine
    for j in range(STEPS):
        for copy in copies[j]:
            copy.wait()
        q = dot(x_held[j], q_held[j])
        kv = dot(x_held[j], kv_held[j])
        if j == 0:
            side_ref[:, :COS] = q
            acc[...] = kv
        else:
            side_ref[:, :COS] += q
            acc[...] += kv
    key = turn(unit(acc[:, :HEAD], gain_ref[...]), side_ref[:, COS:SIN], side_ref[:, SIN:AUX])
    kv_ref[:, :HEAD] = key.astype(jnp.bfloat16)
    kv_ref[:, HEAD:] = acc[:, HEAD:].astype(jnp.bfloat16)


def project(lens, tokens, wq, wk, wv, gain, target):
    near, far = pl.BlockSpec(memory_space=pltpu.VMEM), pl.BlockSpec(memory_space=pltpu.HBM)
    return pl.pallas_call(
        project_kernel,
        in_specs=[pl.BlockSpec(memory_space=pltpu.SMEM)] + [far] * 4 + [near] * 2,
        out_specs=[near] * 2,
        out_shape=[
            jax.ShapeDtypeStruct((ROWS, SIDE), jnp.float32),
            jax.ShapeDtypeStruct((ROWS, 2 * HEAD), jnp.bfloat16),
        ],
        scratch_shapes=[
            pltpu.VMEM((STEPS, ROWS, STEP), jnp.bfloat16),
            pltpu.VMEM((STEPS, STEP, 2 * HEAD), jnp.bfloat16),
            pltpu.VMEM((STEPS, STEP, 2 * HEAD), jnp.bfloat16),
            pltpu.VMEM((ROWS, 2 * HEAD), jnp.float32),
            pltpu.SemaphoreType.DMA((STEPS, 4)),
        ],
        cost_estimate=pl.CostEstimate(
            flops=2 * ROWS * WIDTH * 512, bytes_accessed=12_500_000, transcendentals=0
        ),
        compiler_params=pltpu.CompilerParams(vmem_limit_bytes=20 << 20),
        name="project",
    )(lens, tokens, wq, wk, wv, gain, target)


def adapt_kernel(*refs):
    rows, weights, out = refs[:X], refs[X:X + PARTS], refs[X + PARTS]
    packed, held, sems = refs[X + PARTS + 1:]
    x, z, t = lax.axis_index("x"), lax.axis_index("z"), lax.axis_index("tp")
    copies = [
        pltpu.make_async_copy(
            weights[d].at[pl.ds(n * RANK, RANK), :],
            held.at[lax.rem(z - t + T + NEAR[d] + 4 * n, T)], sems.at[X + sum(SPLIT[:d]) + n])
        for d in range(PARTS) for n in range(SPLIT[d])
    ] + [
        pltpu.make_async_copy(rows[d], packed.at[pl.ds(d * CAP, CAP), :], sems.at[d])
        for d in range(X)
    ]
    for copy in copies:
        copy.start()
    for copy in copies:
        copy.wait()
    low = jnp.zeros((X * CAP, RANK), jnp.float32)
    for w in range(T):
        first = w * SLICE // 128 * 128
        low += dot(packed[:, first:first + PAD], held[w, :, :PAD], 1, 1)
    low = low.astype(jnp.bfloat16)
    for w in range(T):
        delta = dot(low, held[w, :, PAD:]).astype(jnp.bfloat16)
        for d in range(X):
            out[lax.rem(x - d + X, X), w] = delta[d * CAP:(d + 1) * CAP, :]


def adapt(rows, weights):
    return pl.pallas_call(
        adapt_kernel,
        in_specs=[pl.BlockSpec(memory_space=pl.ANY)] * (X + PARTS),
        out_specs=pl.BlockSpec(memory_space=pltpu.VMEM),
        out_shape=jax.ShapeDtypeStruct((X, T, CAP, UP), jnp.bfloat16),
        scratch_shapes=[
            pltpu.VMEM((X * CAP, WIDTH), jnp.bfloat16),
            pltpu.VMEM((T, RANK, PAD + UP), jnp.bfloat16),
            pltpu.SemaphoreType.DMA((X + T,)),
        ],
        compiler_params=pltpu.CompilerParams(vmem_limit_bytes=12 << 20),
        cost_estimate=pl.CostEstimate(
            flops=2 * 128 * RANK * (WIDTH + 2048), bytes_accessed=3_000_000, transcendentals=0
        ),
        name="adapt",
    )(*rows, *weights)


def attend_kernel(delta_hbm, side_hbm, kv0_hbm, kv1_hbm, kv2_hbm, gain_ref, out_ref,
                  delta_ref, side_ref, kv_ref, sems):
    half = ROWS // 2
    pairs = [
        (side_hbm.at[:, pl.ds(AUX, HEAD)], side_ref.at[:, pl.ds(AUX, HEAD)]),
        (delta_hbm, delta_ref),
        (side_hbm.at[:, pl.ds(0, AUX)], side_ref.at[:, pl.ds(0, AUX)]),
    ] + [
        (source.at[:, pl.ds(n * HEAD, HEAD)], kv_ref.at[pl.ds(b * ROWS, ROWS), pl.ds(n * HEAD, HEAD)])
        for b, source in enumerate((kv0_hbm, kv1_hbm, kv2_hbm)) for n in range(2)
    ]
    copies = [
        pltpu.make_async_copy(source, target, sems.at[n])
        for n, (source, target) in enumerate(pairs)
    ]
    for copy in copies:
        copy.start()
    kv_ref[:, 2 * HEAD:] = jnp.ones((3 * ROWS, HEAD), jnp.bfloat16)
    slot = lax.broadcasted_iota(jnp.int32, (ROWS, HEAD), 1)
    copies[0].wait()
    column = jnp.broadcast_to(side_ref[:, SIDE - 1:].astype(jnp.int32), (ROWS, HEAD))
    chosen = jnp.concatenate(
        [(column == slot + c * HEAD).astype(jnp.float32).astype(jnp.bfloat16)
         for c in range(SLOTS // HEAD)], axis=1)
    copies[1].wait()
    delta = dot(chosen, delta_ref[...])
    copies[2].wait()
    query = side_ref[:, :COS] + delta
    gain = gain_ref[...] * (QUERY_SCALE * LOG2E)
    turned = [
        turn(unit(query[:, h * HEAD:(h + 1) * HEAD], gain), side_ref[:, COS:SIN],
             side_ref[:, SIN:AUX]).astype(jnp.bfloat16)
        for h in range(2)
    ]
    for copy in copies[3:]:
        copy.wait()
    for tile in range(2):
        here = slice(tile * half, (tile + 1) * half)
        first, past = tile * half, tile * half + WINDOW + half
        q = jnp.concatenate([turned[0][here], turned[1][here]], axis=0)
        s = dot(q, kv_ref[first:past, :HEAD], 1, 1)
        low = side_ref[here, AUX:AUX + 1].astype(jnp.int32) - first
        at = lax.broadcasted_iota(jnp.int32, (half, WINDOW + half), 1)
        high = WINDOW + lax.broadcasted_iota(jnp.int32, (half, 1), 0)
        allowed = (at >= low) & (at <= high)
        s = jnp.where(jnp.concatenate([allowed, allowed], axis=0), s, -1e30)
        peak = jnp.max(s, axis=-1, keepdims=True)
        weights = jnp.exp2(s - peak).astype(jnp.bfloat16)
        mixed = dot(weights, kv_ref[first:past, HEAD:])
        mixed = (mixed[:, :HEAD] / mixed[:, HEAD:]).astype(jnp.bfloat16)
        out_ref[here, :HEAD] = mixed[:half]
        out_ref[here, HEAD:] = mixed[half:]


def attend(*args):
    near, far = pl.BlockSpec(memory_space=pltpu.VMEM), pl.BlockSpec(memory_space=pl.ANY)
    return pl.pallas_call(
        attend_kernel,
        in_specs=[far] * 5 + [near],
        out_specs=near,
        out_shape=jax.ShapeDtypeStruct((ROWS, 2 * HEAD), jnp.bfloat16),
        scratch_shapes=[
            pltpu.VMEM((SLOTS, UP), jnp.bfloat16),
            pltpu.VMEM((ROWS, SIDE), jnp.float32),
            pltpu.VMEM((3 * ROWS, 3 * HEAD), jnp.bfloat16),
            pltpu.SemaphoreType.DMA((9,)),
        ],
        compiler_params=pltpu.CompilerParams(vmem_limit_bytes=24 << 20),
        cost_estimate=pl.CostEstimate(
            flops=4 * 1024 * 1280 * HEAD, bytes_accessed=4_000_000, transcendentals=1024 * 1280
        ),
        name="attend",
    )(*args)


def layer(
    tokens, query_weight, key_weight, value_weight, query_norm_gain, key_norm_gain,
    adapter_down_weight, adapter_up_weight, token_adapter_index, packed_prompt_length,
):
    tokens, query_weight, key_weight, value_weight = [
        pltpu.with_memory_space_constraint(v, pltpu.HBM)
        for v in (tokens, query_weight, key_weight, value_weight)
    ]
    t = lax.axis_index("tp")
    down = jnp.swapaxes(adapter_down_weight[0], 0, 1)
    shift = lax.rem(t * SLICE, 128)
    carried = functools.reduce(
        lambda other, at: jnp.where(
            shift == at, jnp.pad(down, ((0, 0), (at, PAD + UP - SLICE - at))), other),
        (32, 64, 96), jnp.pad(down, ((0, 0), (0, PAD + UP - SLICE))))
    carried = jnp.where(
        jnp.arange(PAD + UP)[None, :] < PAD, carried,
        jnp.pad(adapter_up_weight[0], ((0, 0), (PAD, 0))))
    single, other = [
        lax.ppermute(
            carried, ("z", "tp"),
            [(a * T + w, (a + w + d) % Z * T + a) for a in range(Z) for w in range(T)])
        for d in (0, 4)
    ]
    double = jnp.concatenate([single, other], axis=0)
    weights = [double] + [
        lax.ppermute(
            double if d in (1, Z - 1) else single, "z", [((i + d) % Z, i) for i in range(Z)])
        for d in NEAR[1:]
    ]
    *rows, target = pack(token_adapter_index.reshape(1, ROWS), tokens)
    rows = [rows[0]] + [
        lax.ppermute(
            rows[d], "x", [(i, (i + d) % X) for i in range(X)])
        for d in range(1, X)
    ]
    side, kv = project(
        packed_prompt_length, tokens, query_weight, key_weight, value_weight,
        key_norm_gain.reshape(1, HEAD), target)
    kv1, kv0 = [
        lax.ppermute(
            kv, ("x", "z"), [(i, i + d) for i in range(X * Z - d)])
        for d in (1, 2)
    ]
    delta = adapt(rows, weights)
    delta = lax.all_to_all(
        delta.reshape(X * T, CAP, UP), ("x", "tp"), 0, 0)
    return attend(
        delta.reshape(SLOTS, UP), side, kv0, kv1, kv, query_norm_gain.reshape(1, HEAD))


def solution(mesh):
    mesh = Mesh(mesh.devices.reshape(X, Z, T), ("x", "z", "tp"))
    seq = ("x", "z")
    in_specs = (
        P(seq, None), P(None, "tp"), P(None, "tp"), P(None, "tp"), P(), P(),
        P(seq, "tp", None), P(seq, None, "tp"), P(seq, None), P(),
    )
    return jax.shard_map(
        layer, mesh=mesh, in_specs=in_specs, out_specs=P(seq, "tp"), check_vma=False)
```

```python
import jax
import jax.numpy as jnp
from jax import lax
from jax.experimental import pallas as pl
from jax.experimental.pallas import tpu as pltpu
from jax.sharding import Mesh, PartitionSpec as P

WINDOW = 1024
QUERY_SCALE = 0.07715167498104596
LOG2E = 1.4426950408889634
X, Z, T = 4, 8, 8
ROWS, WIDTH, HEAD, RANK, CAP = 512, 5376, 128, 64, 32
SLICE = WIDTH // T
PAD = 768
STEP = 768
STEPS = WIDTH // STEP
UP = 256
SLOTS = X * T * CAP
COS, SIN, AUX, SIDE = 0, HEAD, 2 * HEAD, 3 * HEAD
NEAR = (0, 1, Z - 1, 2, Z - 2)
SPLIT = (2, 2, 2, 1, 1)
PARTS = len(NEAR)


def dot(a, b, ca=1, cb=0):
    return lax.dot_general(a, b, (((ca,), (cb,)), ((), ())), preferred_element_type=jnp.float32)


def pack_kernel(idx_hbm, down_hbm, up_hbm, x_ref, out0, out1, out2, out3, target_ref, carried_ref,
                pick, wide, idx_ref, down_ref, held, sems, small_sems):
    small = [
        pltpu.make_async_copy(source, target, small_sems.at[n])
        for n, (source, target) in enumerate((
            (idx_hbm, idx_ref), (down_hbm, down_ref),
            (up_hbm, carried_ref.at[:, pl.ds(PAD, UP)])))
    ]
    for copy in small:
        copy.start()
    copies = [
        pltpu.make_async_copy(x_ref.at[:, pl.ds(j * STEP, STEP)], held.at[j], sems.at[j])
        for j in range(STEPS)
    ]
    for copy in copies:
        copy.start()
    x, t = lax.axis_index("x"), lax.axis_index("tp")
    small[0].wait()
    idx = idx_ref[...]
    named = lax.broadcasted_iota(jnp.int32, (X * T, ROWS), 0) == idx
    earlier = lax.broadcasted_iota(jnp.int32, (ROWS, ROWS), 0) < lax.broadcasted_iota(
        jnp.int32, (ROWS, ROWS), 1
    )
    before = dot(named.astype(jnp.float32).astype(jnp.bfloat16),
                 earlier.astype(jnp.float32).astype(jnp.bfloat16))
    rank = jnp.sum(jnp.where(named, before, 0.0), axis=0, keepdims=True).astype(jnp.int32)
    target = idx * CAP + rank
    target_ref[...] = target
    slot = lax.broadcasted_iota(jnp.int32, (CAP, ROWS), 0)
    for d in range(X):
        adapter = lax.rem(x + d, X) * T + t
        pick[d * CAP:(d + 1) * CAP, :] = (
            (slot + adapter * CAP == target).astype(jnp.float32).astype(jnp.bfloat16)
        )
    small[1].wait()
    wide[:, PAD - 128:] = jnp.zeros((RANK, 128), jnp.float32)
    wide[:, :SLICE] = down_ref[...].astype(jnp.float32)
    carried_ref[:, :PAD] = pltpu.roll(wide[...], lax.rem(t * SLICE, 128), 1).astype(jnp.bfloat16)
    small[2].wait()
    for j in range(STEPS):
        copies[j].wait()
        packed = dot(pick[...], held[j]).astype(jnp.bfloat16)
        for d, out in enumerate((out0, out1, out2, out3)):
            out[:, j * STEP:(j + 1) * STEP] = packed[d * CAP:(d + 1) * CAP, :]


def pack(idx, down, up, tokens):
    row = jax.ShapeDtypeStruct((CAP, WIDTH), jnp.bfloat16)
    return pl.pallas_call(
        pack_kernel,
        in_specs=[pl.BlockSpec(memory_space=pltpu.HBM)] * 4,
        out_specs=[pl.BlockSpec(memory_space=pltpu.VMEM)] * (X + 2),
        out_shape=[row] * X + [
            jax.ShapeDtypeStruct((1, ROWS), jnp.int32),
            jax.ShapeDtypeStruct((RANK, PAD + UP), jnp.bfloat16),
        ],
        scratch_shapes=[
            pltpu.VMEM((X * CAP, ROWS), jnp.bfloat16),
            pltpu.VMEM((RANK, PAD), jnp.float32),
            pltpu.VMEM((1, ROWS), jnp.int32),
            pltpu.VMEM((RANK, SLICE), jnp.bfloat16),
            pltpu.VMEM((STEPS, ROWS, STEP), jnp.bfloat16),
            pltpu.SemaphoreType.DMA((STEPS,)),
            pltpu.SemaphoreType.DMA((3,)),
        ],
        cost_estimate=pl.CostEstimate(
            flops=2 * X * CAP * ROWS * WIDTH, bytes_accessed=7_000_000, transcendentals=0
        ),
        compiler_params=pltpu.CompilerParams(vmem_limit_bytes=12 << 20),
        name="pack",
    )(idx, down, up, tokens)


def unit(field, gain):
    return field / jnp.sqrt(jnp.mean(field * field, axis=-1, keepdims=True) + 1e-06) * gain


def turn(field, cosine, sine):
    return field * cosine + pltpu.roll(field, HEAD // 2, 1) * sine


def fetch(pairs, sems):
    copies = [
        [pltpu.make_async_copy(source, target, sems.at[j, n])
         for n, (source, target) in enumerate(group)]
        for j, group in enumerate(pairs)
    ]
    for group in copies:
        for copy in group:
            copy.start()
    return copies


def keys_kernel(
    lens_ref, x_ref, wk_ref, wv_ref, gain_ref, target_ref, side_ref, kv_ref, x_held, kv_held, acc,
    sems,
):
    part = [pl.ds(j * STEP, STEP) for j in range(STEPS)]
    copies = fetch([
        ((x_ref.at[:, part[j]], x_held.at[j]),
         (wk_ref.at[part[j], :], kv_held.at[j, :, pl.ds(0, HEAD)]),
         (wv_ref.at[part[j], :], kv_held.at[j, :, pl.ds(HEAD, HEAD)]))
        for j in range(STEPS)
    ], sems)
    begin = (lax.axis_index("x") * Z + lax.axis_index("z")) * ROWS
    place = begin + lax.broadcasted_iota(jnp.int32, (ROWS, HEAD), 0)
    start = jnp.zeros((ROWS, HEAD), jnp.int32)
    at = jnp.int32(0)
    for i in range(lens_ref.shape[0]):
        start = jnp.where(place >= at, at, start)
        at = at + lens_ref[i]
    lower = jnp.maximum(start, place - (WINDOW - 1)) - (begin - WINDOW)
    wide = jnp.broadcast_to(target_ref[...].astype(jnp.float32), (HEAD, ROWS))
    lane = lax.broadcasted_iota(jnp.int32, (ROWS, HEAD), 1)
    side_ref[:, AUX:] = jnp.where(lane < HEAD // 2, lower.astype(jnp.float32), jnp.transpose(wide))
    pair = jnp.bitwise_and(lane, HEAD // 2 - 1).astype(jnp.float32)
    angle = place.astype(jnp.float32) * jnp.exp(-(2.0 * pair / HEAD) * jnp.log(jnp.float32(10000.0)))
    sine = jnp.sin(angle)
    side_ref[:, COS:SIN] = jnp.cos(angle)
    side_ref[:, SIN:AUX] = jnp.where(lane < HEAD // 2, -sine, sine)
    for j in range(STEPS):
        for copy in copies[j]:
            copy.wait()
        kv = dot(x_held[j], kv_held[j])
        if j == 0:
            acc[...] = kv
        else:
            acc[...] += kv
    key = turn(unit(acc[:, :HEAD], gain_ref[...]), side_ref[:, COS:SIN], side_ref[:, SIN:AUX])
    kv_ref[:, :HEAD] = key.astype(jnp.bfloat16)
    kv_ref[:, HEAD:] = acc[:, HEAD:].astype(jnp.bfloat16)


def project_keys(lens, tokens, wk, wv, gain, target):
    near, far = pl.BlockSpec(memory_space=pltpu.VMEM), pl.BlockSpec(memory_space=pltpu.HBM)
    return pl.pallas_call(
        keys_kernel,
        in_specs=[pl.BlockSpec(memory_space=pltpu.SMEM)] + [far] * 3 + [near] * 2,
        out_specs=[near] * 2,
        out_shape=[
            jax.ShapeDtypeStruct((ROWS, SIDE), jnp.float32),
            jax.ShapeDtypeStruct((ROWS, 2 * HEAD), jnp.bfloat16),
        ],
        scratch_shapes=[
            pltpu.VMEM((STEPS, ROWS, STEP), jnp.bfloat16),
            pltpu.VMEM((STEPS, STEP, 2 * HEAD), jnp.bfloat16),
            pltpu.VMEM((ROWS, 2 * HEAD), jnp.float32),
            pltpu.SemaphoreType.DMA((STEPS, 3)),
        ],
        compiler_params=pltpu.CompilerParams(vmem_limit_bytes=16 << 20),
        cost_estimate=pl.CostEstimate(
            flops=2 * ROWS * WIDTH * 256, bytes_accessed=9_500_000, transcendentals=0
        ),
        name="project_keys",
    )(lens, tokens, wk, wv, gain, target)


def queries_kernel(x_ref, wq_ref, q_ref, x_held, q_held, sems):
    part = [pl.ds(j * STEP, STEP) for j in range(STEPS)]
    copies = fetch([
        ((x_ref.at[:, part[j]], x_held.at[j]), (wq_ref.at[part[j], :], q_held.at[j]))
        for j in range(STEPS)
    ], sems)
    for j in range(STEPS):
        for copy in copies[j]:
            copy.wait()
        q = dot(x_held[j], q_held[j])
        if j == 0:
            q_ref[...] = q
        else:
            q_ref[...] += q


def project_queries(tokens, wq):
    near, far = pl.BlockSpec(memory_space=pltpu.VMEM), pl.BlockSpec(memory_space=pltpu.HBM)
    return pl.pallas_call(
        queries_kernel,
        in_specs=[far] * 2,
        out_specs=near,
        out_shape=jax.ShapeDtypeStruct((ROWS, 2 * HEAD), jnp.float32),
        scratch_shapes=[
            pltpu.VMEM((STEPS, ROWS, STEP), jnp.bfloat16),
            pltpu.VMEM((STEPS, STEP, 2 * HEAD), jnp.bfloat16),
            pltpu.SemaphoreType.DMA((STEPS, 2)),
        ],
        compiler_params=pltpu.CompilerParams(vmem_limit_bytes=16 << 20),
        cost_estimate=pl.CostEstimate(
            flops=2 * ROWS * WIDTH * 256, bytes_accessed=8_800_000, transcendentals=0
        ),
        name="project_queries",
    )(tokens, wq)


def adapt_kernel(*refs):
    rows, weights, out = refs[:X], refs[X:X + PARTS], refs[X + PARTS]
    packed, held, sems = refs[X + PARTS + 1:]
    x, z, t = lax.axis_index("x"), lax.axis_index("z"), lax.axis_index("tp")
    copies = [
        pltpu.make_async_copy(
            weights[d].at[pl.ds(n * RANK, RANK), :],
            held.at[lax.rem(z - t + T + NEAR[d] + 4 * n, T)], sems.at[X + sum(SPLIT[:d]) + n])
        for d in range(PARTS) for n in range(SPLIT[d])
    ] + [
        pltpu.make_async_copy(rows[d], packed.at[pl.ds(d * CAP, CAP), :], sems.at[d])
        for d in range(X)
    ]
    for copy in copies:
        copy.start()
    for copy in copies:
        copy.wait()
    chunks = [(w, n * 256) for w in range(T) for n in range(PAD // 256)]
    groups = len(chunks) // 4
    left, right = [], []
    for j in range(4):
        mine = chunks[j * groups:(j + 1) * groups]
        firsts = [w * SLICE // 128 * 128 + n for w, n in mine]
        left.append(jnp.concatenate([packed[:, at:at + 256] for at in firsts], axis=1))
        right.append(jnp.concatenate([held[w, :, n:n + 256] for w, n in mine], axis=1))
    low = dot(jnp.concatenate(left, axis=0), jnp.concatenate(right, axis=0), 1, 1)
    low = sum(
        low[j * X * CAP:(j + 1) * X * CAP, j * RANK:(j + 1) * RANK] for j in range(4))
    low = low.astype(jnp.bfloat16)
    for w in range(T):
        delta = dot(low, held[w, :, PAD:]).astype(jnp.bfloat16)
        for d in range(X):
            out[lax.rem(x - d + X, X), w] = delta[d * CAP:(d + 1) * CAP, :]


def adapt(rows, weights):
    return pl.pallas_call(
        adapt_kernel,
        in_specs=[pl.BlockSpec(memory_space=pl.ANY)] * (X + PARTS),
        out_specs=pl.BlockSpec(memory_space=pltpu.VMEM),
        out_shape=jax.ShapeDtypeStruct((X, T, CAP, UP), jnp.bfloat16),
        scratch_shapes=[
            pltpu.VMEM((X * CAP, WIDTH), jnp.bfloat16),
            pltpu.VMEM((T, RANK, PAD + UP), jnp.bfloat16),
            pltpu.SemaphoreType.DMA((X + T,)),
        ],
        compiler_params=pltpu.CompilerParams(vmem_limit_bytes=12 << 20),
        cost_estimate=pl.CostEstimate(
            flops=2 * 128 * RANK * (WIDTH + 2048), bytes_accessed=3_000_000, transcendentals=0
        ),
        name="adapt",
    )(*rows, *weights)


def attend_kernel(delta_hbm, q_hbm, side_hbm, kv0_hbm, kv1_hbm, kv2_hbm, gain_ref, out_ref,
                  delta_ref, q_ref, side_ref, kv_ref, sems):
    half = ROWS // 2
    pairs = [
        (side_hbm.at[:, pl.ds(AUX, HEAD)], side_ref.at[:, pl.ds(AUX, HEAD)]),
        (delta_hbm, delta_ref),
        (q_hbm, q_ref),
        (side_hbm.at[:, pl.ds(0, AUX)], side_ref.at[:, pl.ds(0, AUX)]),
    ] + [
        (source.at[:, pl.ds(n * HEAD, HEAD)], kv_ref.at[pl.ds(b * ROWS, ROWS), pl.ds(n * HEAD, HEAD)])
        for b, source in enumerate((kv0_hbm, kv1_hbm, kv2_hbm)) for n in range(2)
    ]
    copies = [
        pltpu.make_async_copy(source, target, sems.at[n])
        for n, (source, target) in enumerate(pairs)
    ]
    for copy in copies:
        copy.start()
    kv_ref[:, 2 * HEAD:] = jnp.ones((3 * ROWS, HEAD), jnp.bfloat16)
    slot = lax.broadcasted_iota(jnp.int32, (ROWS, HEAD), 1)
    copies[0].wait()
    column = jnp.broadcast_to(side_ref[:, SIDE - 1:].astype(jnp.int32), (ROWS, HEAD))
    chosen = jnp.concatenate(
        [(column == slot + c * HEAD).astype(jnp.float32).astype(jnp.bfloat16)
         for c in range(SLOTS // HEAD)], axis=1)
    copies[1].wait()
    delta = dot(chosen, delta_ref[...])
    copies[2].wait()
    copies[3].wait()
    query = q_ref[...] + delta
    gain = gain_ref[...] * (QUERY_SCALE * LOG2E)
    turned = [
        turn(unit(query[:, h * HEAD:(h + 1) * HEAD], gain), side_ref[:, COS:SIN],
             side_ref[:, SIN:AUX]).astype(jnp.bfloat16)
        for h in range(2)
    ]
    for copy in copies[4:]:
        copy.wait()
    for tile in range(2):
        here = slice(tile * half, (tile + 1) * half)
        first, past = tile * half, tile * half + WINDOW + half
        q = jnp.concatenate([turned[0][here], turned[1][here]], axis=0)
        s = dot(q, kv_ref[first:past, :HEAD], 1, 1)
        low = side_ref[here, AUX:AUX + 1].astype(jnp.int32) - first
        at = lax.broadcasted_iota(jnp.int32, (half, WINDOW + half), 1)
        high = WINDOW + lax.broadcasted_iota(jnp.int32, (half, 1), 0)
        allowed = (at >= low) & (at <= high)
        s = jnp.where(jnp.concatenate([allowed, allowed], axis=0), s, -1e30)
        peak = jnp.max(s, axis=-1, keepdims=True)
        weights = jnp.exp2(s - peak).astype(jnp.bfloat16)
        mixed = dot(weights, kv_ref[first:past, HEAD:])
        mixed = (mixed[:, :HEAD] / mixed[:, HEAD:]).astype(jnp.bfloat16)
        out_ref[here, :HEAD] = mixed[:half]
        out_ref[here, HEAD:] = mixed[half:]


def attend(*args):
    near, far = pl.BlockSpec(memory_space=pltpu.VMEM), pl.BlockSpec(memory_space=pl.ANY)
    return pl.pallas_call(
        attend_kernel,
        in_specs=[far] * 6 + [near],
        out_specs=near,
        out_shape=jax.ShapeDtypeStruct((ROWS, 2 * HEAD), jnp.bfloat16),
        scratch_shapes=[
            pltpu.VMEM((SLOTS, UP), jnp.bfloat16),
            pltpu.VMEM((ROWS, 2 * HEAD), jnp.float32),
            pltpu.VMEM((ROWS, SIDE), jnp.float32),
            pltpu.VMEM((3 * ROWS, 3 * HEAD), jnp.bfloat16),
            pltpu.SemaphoreType.DMA((10,)),
        ],
        compiler_params=pltpu.CompilerParams(vmem_limit_bytes=24 << 20),
        cost_estimate=pl.CostEstimate(
            flops=4 * 1024 * 1280 * HEAD, bytes_accessed=4_000_000, transcendentals=1024 * 1280
        ),
        name="attend",
    )(*args)


def layer(
    tokens, query_weight, key_weight, value_weight, query_norm_gain, key_norm_gain,
    adapter_down_weight, adapter_up_weight, token_adapter_index, packed_prompt_length,
):
    down = jnp.swapaxes(adapter_down_weight[0], 0, 1)
    index = token_adapter_index.reshape(1, ROWS)
    tokens, query_weight, key_weight, value_weight, down, up, index = [
        pltpu.with_memory_space_constraint(v, pltpu.HBM)
        for v in (tokens, query_weight, key_weight, value_weight, down, adapter_up_weight[0], index)
    ]
    *rows, target, carried = pack(
        index, down, up, tokens)
    single, other = [
        lax.ppermute(
            carried, ("z", "tp"),
            [(a * T + w, (a + w + d) % Z * T + a) for a in range(Z) for w in range(T)])
        for d in (0, 4)
    ]
    double = jnp.concatenate([single, other], axis=0)
    weights = [double] + [
        lax.ppermute(
            double if d in (1, Z - 1) else single, "z", [((i + d) % Z, i) for i in range(Z)])
        for d in NEAR[1:]
    ]
    rows = [rows[0]] + [
        lax.ppermute(
            rows[d], "x", [(i, (i + d) % X) for i in range(X)])
        for d in range(1, X)
    ]
    side, kv = project_keys(
        packed_prompt_length, tokens, key_weight, value_weight,
        key_norm_gain.reshape(1, HEAD), target)
    query = project_queries(tokens, query_weight)
    kv1, kv0 = [
        lax.ppermute(
            kv, ("x", "z"), [(i, i + d) for i in range(X * Z - d)])
        for d in (1, 2)
    ]
    delta = adapt(rows, weights)
    delta = lax.all_to_all(
        delta.reshape(X * T, CAP, UP), ("x", "tp"), 0, 0)
    return attend(
        delta.reshape(SLOTS, UP), query, side, kv0, kv1, kv, query_norm_gain.reshape(1, HEAD))


def solution(mesh):
    mesh = Mesh(mesh.devices.reshape(X, Z, T), ("x", "z", "tp"))
    seq = ("x", "z")
    in_specs = (
        P(seq, None), P(None, "tp"), P(None, "tp"), P(None, "tp"), P(), P(),
        P(seq, "tp", None), P(seq, None, "tp"), P(seq, None), P(),
    )
    return jax.shard_map(
        layer, mesh=mesh, in_specs=in_specs, out_specs=P(seq, "tp"), check_vma=False)
```

```python
import jax
import jax.numpy as jnp
from jax import lax
from jax.experimental import pallas as pl
from jax.experimental.pallas import tpu as pltpu
from jax.sharding import Mesh, PartitionSpec as P

WINDOW = 1024
QUERY_SCALE = 0.07715167498104596
LOG2E = 1.4426950408889634
X, Z, T = 4, 8, 8
ROWS, WIDTH, HEAD, RANK, CAP = 512, 5376, 128, 64, 32
SLICE = WIDTH // T
PAD = 768
STEP = 768
STEPS = WIDTH // STEP
UP = 256
SLOTS = X * T * CAP
COS, SIN, AUX, SIDE = 0, HEAD, 2 * HEAD, 3 * HEAD
NEAR = (0, 1, Z - 1, 2, Z - 2)
SPLIT = (2, 2, 2, 1, 1)
PARTS = len(NEAR)


def dot(a, b, ca=1, cb=0):
    return lax.dot_general(a, b, (((ca,), (cb,)), ((), ())), preferred_element_type=jnp.float32)


def unit(field, gain):
    return field / jnp.sqrt(jnp.mean(field * field, axis=-1, keepdims=True) + 1e-06) * gain


def turn(field, cosine, sine):
    return field * cosine + pltpu.roll(field, HEAD // 2, 1) * sine


def fetch(pairs, sems):
    copies = [
        [pltpu.make_async_copy(source, target, sems.at[j, n])
         for n, (source, target) in enumerate(group)]
        for j, group in enumerate(pairs)
    ]
    for group in copies:
        for copy in group:
            copy.start()
    return copies


def front_kernel(
    lens_ref, gain_ref, idx_hbm, down_hbm, up_hbm, x_hbm, wk_hbm, wv_hbm,
    out0, out1, out2, out3, carried_ref, side_ref, kv_ref,
    pick, wide, idx_ref, down_ref, x_held, kv_held, acc, small_sems, sems,
):
    part = [pl.ds(j * STEP, STEP) for j in range(STEPS)]
    small = [
        pltpu.make_async_copy(source, target, small_sems.at[n])
        for n, (source, target) in enumerate((
            (idx_hbm, idx_ref), (down_hbm, down_ref),
            (up_hbm, carried_ref.at[:, pl.ds(PAD, UP)])))
    ]
    for copy in small:
        copy.start()
    copies = fetch([
        ((x_hbm.at[:, part[j]], x_held.at[j]),
         (wk_hbm.at[part[j], :], kv_held.at[j, :, pl.ds(0, HEAD)]),
         (wv_hbm.at[part[j], :], kv_held.at[j, :, pl.ds(HEAD, HEAD)]))
        for j in range(STEPS)
    ], sems)
    x, z, t = lax.axis_index("x"), lax.axis_index("z"), lax.axis_index("tp")
    small[0].wait()
    idx = idx_ref[...]
    named = lax.broadcasted_iota(jnp.int32, (X * T, ROWS), 0) == idx
    earlier = lax.broadcasted_iota(jnp.int32, (ROWS, ROWS), 0) < lax.broadcasted_iota(
        jnp.int32, (ROWS, ROWS), 1
    )
    before = dot(named.astype(jnp.float32).astype(jnp.bfloat16),
                 earlier.astype(jnp.float32).astype(jnp.bfloat16))
    rank = jnp.sum(jnp.where(named, before, 0.0), axis=0, keepdims=True).astype(jnp.int32)
    target = idx * CAP + rank
    slot = lax.broadcasted_iota(jnp.int32, (CAP, ROWS), 0)
    for d in range(X):
        adapter = lax.rem(x + d, X) * T + t
        pick[d * CAP:(d + 1) * CAP, :] = (
            (slot + adapter * CAP == target).astype(jnp.float32).astype(jnp.bfloat16)
        )
    small[1].wait()
    wide[:, PAD - 128:] = jnp.zeros((RANK, 128), jnp.float32)
    wide[:, :SLICE] = down_ref[...].astype(jnp.float32)
    carried_ref[:, :PAD] = pltpu.roll(wide[...], lax.rem(t * SLICE, 128), 1).astype(jnp.bfloat16)
    small[2].wait()
    begin = (x * Z + z) * ROWS
    place = begin + lax.broadcasted_iota(jnp.int32, (ROWS, HEAD), 0)
    start = jnp.zeros((ROWS, HEAD), jnp.int32)
    at = jnp.int32(0)
    for i in range(lens_ref.shape[0]):
        start = jnp.where(place >= at, at, start)
        at = at + lens_ref[i]
    lower = jnp.maximum(start, place - (WINDOW - 1)) - (begin - WINDOW)
    column = jnp.broadcast_to(target.astype(jnp.float32), (HEAD, ROWS))
    lane = lax.broadcasted_iota(jnp.int32, (ROWS, HEAD), 1)
    side_ref[:, AUX:] = jnp.where(lane < HEAD // 2, lower.astype(jnp.float32), jnp.transpose(column))
    pair = jnp.bitwise_and(lane, HEAD // 2 - 1).astype(jnp.float32)
    angle = place.astype(jnp.float32) * jnp.exp(-(2.0 * pair / HEAD) * jnp.log(jnp.float32(10000.0)))
    sine = jnp.sin(angle)
    side_ref[:, COS:SIN] = jnp.cos(angle)
    side_ref[:, SIN:AUX] = jnp.where(lane < HEAD // 2, -sine, sine)
    for j in range(STEPS):
        for copy in copies[j]:
            copy.wait()
        packed = dot(pick[...], x_held[j]).astype(jnp.bfloat16)
        for d, out in enumerate((out0, out1, out2, out3)):
            out[:, j * STEP:(j + 1) * STEP] = packed[d * CAP:(d + 1) * CAP, :]
        kv = dot(x_held[j], kv_held[j])
        if j == 0:
            acc[...] = kv
        else:
            acc[...] += kv
    key = turn(unit(acc[:, :HEAD], gain_ref[...]), side_ref[:, COS:SIN], side_ref[:, SIN:AUX])
    kv_ref[:, :HEAD] = key.astype(jnp.bfloat16)
    kv_ref[:, HEAD:] = acc[:, HEAD:].astype(jnp.bfloat16)


def front(lens, gain, idx, down, up, tokens, wk, wv):
    near, far = pl.BlockSpec(memory_space=pltpu.VMEM), pl.BlockSpec(memory_space=pltpu.HBM)
    return pl.pallas_call(
        front_kernel,
        in_specs=[pl.BlockSpec(memory_space=pltpu.SMEM), near] + [far] * 6,
        out_specs=[near] * (X + 3),
        out_shape=[jax.ShapeDtypeStruct((CAP, WIDTH), jnp.bfloat16)] * X + [
            jax.ShapeDtypeStruct((RANK, PAD + UP), jnp.bfloat16),
            jax.ShapeDtypeStruct((ROWS, SIDE), jnp.float32),
            jax.ShapeDtypeStruct((ROWS, 2 * HEAD), jnp.bfloat16),
        ],
        scratch_shapes=[
            pltpu.VMEM((X * CAP, ROWS), jnp.bfloat16),
            pltpu.VMEM((RANK, PAD), jnp.float32),
            pltpu.VMEM((1, ROWS), jnp.int32),
            pltpu.VMEM((RANK, SLICE), jnp.bfloat16),
            pltpu.VMEM((STEPS, ROWS, STEP), jnp.bfloat16),
            pltpu.VMEM((STEPS, STEP, 2 * HEAD), jnp.bfloat16),
            pltpu.VMEM((ROWS, 2 * HEAD), jnp.float32),
            pltpu.SemaphoreType.DMA((3,)),
            pltpu.SemaphoreType.DMA((STEPS, 3)),
        ],
        compiler_params=pltpu.CompilerParams(vmem_limit_bytes=18 << 20),
        cost_estimate=pl.CostEstimate(
            flops=2 * ROWS * WIDTH * 384, bytes_accessed=10_000_000, transcendentals=0
        ),
        name="front",
    )(lens, gain, idx, down, up, tokens, wk, wv)


def queries_kernel(x_ref, wq_ref, q_ref, x_held, q_held, sems):
    part = [pl.ds(j * STEP, STEP) for j in range(STEPS)]
    copies = fetch([
        ((x_ref.at[:, part[j]], x_held.at[j]), (wq_ref.at[part[j], :], q_held.at[j]))
        for j in range(STEPS)
    ], sems)
    for j in range(STEPS):
        for copy in copies[j]:
            copy.wait()
        q = dot(x_held[j], q_held[j])
        if j == 0:
            q_ref[...] = q
        else:
            q_ref[...] += q


def project_queries(tokens, wq):
    near, far = pl.BlockSpec(memory_space=pltpu.VMEM), pl.BlockSpec(memory_space=pltpu.HBM)
    return pl.pallas_call(
        queries_kernel,
        in_specs=[far] * 2,
        out_specs=near,
        out_shape=jax.ShapeDtypeStruct((ROWS, 2 * HEAD), jnp.float32),
        scratch_shapes=[
            pltpu.VMEM((STEPS, ROWS, STEP), jnp.bfloat16),
            pltpu.VMEM((STEPS, STEP, 2 * HEAD), jnp.bfloat16),
            pltpu.SemaphoreType.DMA((STEPS, 2)),
        ],
        compiler_params=pltpu.CompilerParams(vmem_limit_bytes=16 << 20),
        cost_estimate=pl.CostEstimate(
            flops=2 * ROWS * WIDTH * 256, bytes_accessed=8_800_000, transcendentals=0
        ),
        name="project_queries",
    )(tokens, wq)


def adapt_kernel(*refs):
    rows, weights, out = refs[:X], refs[X:X + PARTS], refs[X + PARTS]
    held = refs[X + PARTS + 1]
    x, z, t = lax.axis_index("x"), lax.axis_index("z"), lax.axis_index("tp")
    for d in range(PARTS):
        for n in range(SPLIT[d]):
            held[lax.rem(z - t + T + NEAR[d] + 4 * n, T)] = weights[d][n * RANK:(n + 1) * RANK, :]
    packed = jnp.concatenate([r[...] for r in rows], axis=0)
    chunks = [(w, n * 256) for w in range(T) for n in range(PAD // 256)]
    groups = len(chunks) // 4
    left, right = [], []
    for j in range(4):
        mine = chunks[j * groups:(j + 1) * groups]
        firsts = [w * SLICE // 128 * 128 + n for w, n in mine]
        left.append(jnp.concatenate([packed[:, at:at + 256] for at in firsts], axis=1))
        right.append(jnp.concatenate([held[w, :, n:n + 256] for w, n in mine], axis=1))
    low = dot(jnp.concatenate(left, axis=0), jnp.concatenate(right, axis=0), 1, 1)
    low = sum(
        low[j * X * CAP:(j + 1) * X * CAP, j * RANK:(j + 1) * RANK] for j in range(4))
    low = low.astype(jnp.bfloat16)
    for w in range(T):
        delta = dot(low, held[w, :, PAD:]).astype(jnp.bfloat16)
        for d in range(X):
            out[lax.rem(x - d + X, X), w] = delta[d * CAP:(d + 1) * CAP, :]


def adapt(rows, weights):
    return pl.pallas_call(
        adapt_kernel,
        in_specs=[pl.BlockSpec(memory_space=pltpu.VMEM)] * (X + PARTS),
        out_specs=pl.BlockSpec(memory_space=pltpu.VMEM),
        out_shape=jax.ShapeDtypeStruct((X, T, CAP, UP), jnp.bfloat16),
        scratch_shapes=[
            pltpu.VMEM((T, RANK, PAD + UP), jnp.bfloat16),
        ],
        compiler_params=pltpu.CompilerParams(vmem_limit_bytes=12 << 20),
        cost_estimate=pl.CostEstimate(
            flops=2 * 128 * RANK * (WIDTH + 2048), bytes_accessed=3_000_000, transcendentals=0
        ),
        name="adapt",
    )(*rows, *weights)


def attend_kernel(delta_ref, q_ref, side_ref, kv0, kv1, kv2, gain_ref, out_ref, kv_ref):
    half = ROWS // 2
    for b, source in enumerate((kv0, kv1, kv2)):
        kv_ref[b * ROWS:(b + 1) * ROWS, :2 * HEAD] = source[...]
    kv_ref[:, 2 * HEAD:] = jnp.ones((3 * ROWS, HEAD), jnp.bfloat16)
    slot = lax.broadcasted_iota(jnp.int32, (ROWS, HEAD), 1)
    column = jnp.broadcast_to(side_ref[:, SIDE - 1:].astype(jnp.int32), (ROWS, HEAD))
    chosen = jnp.concatenate(
        [(column == slot + c * HEAD).astype(jnp.float32).astype(jnp.bfloat16)
         for c in range(SLOTS // HEAD)], axis=1)
    delta = dot(chosen, delta_ref[...])
    query = q_ref[...] + delta
    gain = gain_ref[...] * (QUERY_SCALE * LOG2E)
    turned = [
        turn(unit(query[:, h * HEAD:(h + 1) * HEAD], gain), side_ref[:, COS:SIN],
             side_ref[:, SIN:AUX]).astype(jnp.bfloat16)
        for h in range(2)
    ]
    for tile in range(2):
        here = slice(tile * half, (tile + 1) * half)
        first, past = tile * half, tile * half + WINDOW + half
        q = jnp.concatenate([turned[0][here], turned[1][here]], axis=0)
        s = dot(q, kv_ref[first:past, :HEAD], 1, 1)
        low = side_ref[here, AUX:AUX + 1].astype(jnp.int32) - first
        at = lax.broadcasted_iota(jnp.int32, (half, WINDOW + half), 1)
        high = WINDOW + lax.broadcasted_iota(jnp.int32, (half, 1), 0)
        allowed = (at >= low) & (at <= high)
        s = jnp.where(jnp.concatenate([allowed, allowed], axis=0), s, -1e30)
        peak = jnp.max(s, axis=-1, keepdims=True)
        weights = jnp.exp2(s - peak).astype(jnp.bfloat16)
        mixed = dot(weights, kv_ref[first:past, HEAD:])
        mixed = (mixed[:, :HEAD] / mixed[:, HEAD:]).astype(jnp.bfloat16)
        out_ref[here, :HEAD] = mixed[:half]
        out_ref[here, HEAD:] = mixed[half:]


def attend(*args):
    near = pl.BlockSpec(memory_space=pltpu.VMEM)
    return pl.pallas_call(
        attend_kernel,
        in_specs=[near] * 7,
        out_specs=near,
        out_shape=jax.ShapeDtypeStruct((ROWS, 2 * HEAD), jnp.bfloat16),
        scratch_shapes=[
            pltpu.VMEM((3 * ROWS, 3 * HEAD), jnp.bfloat16),
        ],
        compiler_params=pltpu.CompilerParams(vmem_limit_bytes=24 << 20),
        cost_estimate=pl.CostEstimate(
            flops=4 * 1024 * 1280 * HEAD, bytes_accessed=4_000_000, transcendentals=1024 * 1280
        ),
        name="attend",
    )(*args)


def layer(
    tokens, query_weight, key_weight, value_weight, query_norm_gain, key_norm_gain,
    adapter_down_weight, adapter_up_weight, token_adapter_index, packed_prompt_length,
):
    down = jnp.swapaxes(adapter_down_weight[0], 0, 1)
    index = token_adapter_index.reshape(1, ROWS)
    key_gain = key_norm_gain.reshape(1, HEAD)
    (tokens, query_weight, key_weight, value_weight, down, up, index, key_gain,
     packed_prompt_length) = [
        pltpu.with_memory_space_constraint(v, pltpu.HBM)
        for v in (tokens, query_weight, key_weight, value_weight, down, adapter_up_weight[0],
                  index, key_gain, packed_prompt_length)
    ]
    *rows, carried, side, kv = front(
        packed_prompt_length, key_gain, index, down, up,
        tokens, key_weight, value_weight)
    single, other = [
        lax.ppermute(
            carried, ("z", "tp"),
            [(a * T + w, (a + w + d) % Z * T + a) for a in range(Z) for w in range(T)])
        for d in (0, 4)
    ]
    double = jnp.concatenate([single, other], axis=0)
    weights = [double] + [
        lax.ppermute(
            double if d in (1, Z - 1) else single, "z", [((i + d) % Z, i) for i in range(Z)])
        for d in NEAR[1:]
    ]
    rows = [rows[0]] + [
        lax.ppermute(
            rows[d], "x", [(i, (i + d) % X) for i in range(X)])
        for d in range(1, X)
    ]
    query = project_queries(tokens, query_weight)
    kv1, kv0 = [
        lax.ppermute(
            kv, ("x", "z"), [(i, i + d) for i in range(X * Z - d)])
        for d in (1, 2)
    ]
    delta = adapt(rows, weights)
    delta = lax.all_to_all(
        delta.reshape(X * T, CAP, UP), ("x", "tp"), 0, 0)
    return attend(
        delta.reshape(SLOTS, UP), query, side, kv0, kv1, kv, query_norm_gain.reshape(1, HEAD))


def solution(mesh):
    mesh = Mesh(mesh.devices.reshape(X, Z, T), ("x", "z", "tp"))
    seq = ("x", "z")
    in_specs = (
        P(seq, None), P(None, "tp"), P(None, "tp"), P(None, "tp"), P(), P(),
        P(seq, "tp", None), P(seq, None, "tp"), P(seq, None), P(),
    )
    return jax.shard_map(
        layer, mesh=mesh, in_specs=in_specs, out_specs=P(seq, "tp"), check_vma=False)
```

```python
import functools
import jax
import jax.numpy as jnp
from jax import lax
from jax.experimental import pallas as pl
from jax.experimental.pallas import tpu as pltpu
from jax.sharding import Mesh, PartitionSpec as P

WINDOW = 1024
QUERY_SCALE = 0.07715167498104596
LOG2E = 1.4426950408889634
TILES = 4
X, Z, T = 4, 8, 8
ROWS, WIDTH, HEAD, RANK, CAP = 512, 5376, 128, 64, 32
SLICE = WIDTH // T
PAD = 768
STEP = 768
STEPS = WIDTH // STEP
UP = 256
SLOTS = X * T * CAP
COS, SIN, AUX, SIDE = 0, HEAD, 2 * HEAD, 3 * HEAD
NEAR = (0, 1, Z - 1, 2, Z - 2)
SPLIT = (2, 2, 2, 1, 1)
PARTS = len(NEAR)


def dot(a, b, ca=1, cb=0):
    return lax.dot_general(a, b, (((ca,), (cb,)), ((), ())), preferred_element_type=jnp.float32)


def pack_kernel(idx_hbm, x_ref, out0, out1, out2, out3, target_ref, pick, idx_ref, held, sems,
                idx_sem):
    small = pltpu.make_async_copy(idx_hbm, idx_ref, idx_sem.at[0])
    small.start()
    copies = [
        pltpu.make_async_copy(x_ref.at[:, pl.ds(j * STEP, STEP)], held.at[j], sems.at[j])
        for j in range(STEPS)
    ]
    for copy in copies:
        copy.start()
    x, t = lax.axis_index("x"), lax.axis_index("tp")
    small.wait()
    idx = idx_ref[...]
    named = lax.broadcasted_iota(jnp.int32, (X * T, ROWS), 0) == idx
    earlier = lax.broadcasted_iota(jnp.int32, (ROWS, ROWS), 0) < lax.broadcasted_iota(
        jnp.int32, (ROWS, ROWS), 1
    )
    before = dot(named.astype(jnp.float32).astype(jnp.bfloat16),
                 earlier.astype(jnp.float32).astype(jnp.bfloat16))
    rank = jnp.sum(jnp.where(named, before, 0.0), axis=0, keepdims=True).astype(jnp.int32)
    target = idx * CAP + rank
    target_ref[...] = target
    slot = lax.broadcasted_iota(jnp.int32, (CAP, ROWS), 0)
    for d in range(X):
        adapter = lax.rem(x + d, X) * T + t
        pick[d * CAP:(d + 1) * CAP, :] = (
            (slot + adapter * CAP == target).astype(jnp.float32).astype(jnp.bfloat16)
        )
    for j in range(STEPS):
        copies[j].wait()
        packed = dot(pick[...], held[j]).astype(jnp.bfloat16)
        for d, out in enumerate((out0, out1, out2, out3)):
            out[:, j * STEP:(j + 1) * STEP] = packed[d * CAP:(d + 1) * CAP, :]


def pack(idx, tokens):
    row = jax.ShapeDtypeStruct((CAP, WIDTH), jnp.bfloat16)
    return pl.pallas_call(
        pack_kernel,
        in_specs=[pl.BlockSpec(memory_space=pltpu.HBM)] * 2,
        out_specs=[pl.BlockSpec(memory_space=pltpu.VMEM)] * (X + 1),
        out_shape=[row] * X + [
            jax.ShapeDtypeStruct((1, ROWS), jnp.int32),
        ],
        scratch_shapes=[
            pltpu.VMEM((X * CAP, ROWS), jnp.bfloat16),
            pltpu.VMEM((1, ROWS), jnp.int32),
            pltpu.VMEM((STEPS, ROWS, STEP), jnp.bfloat16),
            pltpu.SemaphoreType.DMA((STEPS,)),
            pltpu.SemaphoreType.DMA((1,)),
        ],
        cost_estimate=pl.CostEstimate(
            flops=2 * X * CAP * ROWS * WIDTH, bytes_accessed=7_000_000, transcendentals=0
        ),
        compiler_params=pltpu.CompilerParams(vmem_limit_bytes=12 << 20),
        name="pack",
    )(idx, tokens)


def unit(field, gain):
    return field / jnp.sqrt(jnp.mean(field * field, axis=-1, keepdims=True) + 1e-06) * gain


def turn(field, cosine, sine):
    return field * cosine + pltpu.roll(field, HEAD // 2, 1) * sine


def fetch(pairs, sems):
    copies = [
        [pltpu.make_async_copy(source, target, sems.at[j, n])
         for n, (source, target) in enumerate(group)]
        for j, group in enumerate(pairs)
    ]
    for group in copies:
        for copy in group:
            copy.start()
    return copies


def keys_kernel(
    lens_ref, x_ref, wk_ref, wv_ref, gain_ref, target_ref, side_ref, kv_ref, x_held, kv_held, acc,
    sems,
):
    part = [pl.ds(j * STEP, STEP) for j in range(STEPS)]
    copies = fetch([
        ((x_ref.at[:, part[j]], x_held.at[j]),
         (wk_ref.at[part[j], :], kv_held.at[j, :, pl.ds(0, HEAD)]),
         (wv_ref.at[part[j], :], kv_held.at[j, :, pl.ds(HEAD, HEAD)]))
        for j in range(STEPS)
    ], sems)
    begin = (lax.axis_index("x") * Z + lax.axis_index("z")) * ROWS
    wide = jnp.broadcast_to(target_ref[...].astype(jnp.float32), (HEAD, ROWS))
    side_ref[:, AUX:] = jnp.transpose(wide)
    for j in range(STEPS):
        for copy in copies[j]:
            copy.wait()
        kv = dot(x_held[j], kv_held[j])
        if j == 0:
            acc[...] = kv
        else:
            acc[...] += kv
        first, past = ROWS // 8 * j // STEPS * 8, ROWS // 8 * (j + 1) // STEPS * 8
        shape = (past - first, HEAD)
        place = begin + first + lax.broadcasted_iota(jnp.int32, shape, 0)
        start = jnp.zeros(shape, jnp.int32)
        at = jnp.int32(0)
        for i in range(lens_ref.shape[0]):
            start = jnp.where(place >= at, at, start)
            at = at + lens_ref[i]
        lower = jnp.maximum(start, place - (WINDOW - 1)) - (begin - WINDOW)
        lane = lax.broadcasted_iota(jnp.int32, shape, 1)
        side_ref[first:past, AUX:] = jnp.where(
            lane < HEAD // 2, lower.astype(jnp.float32), side_ref[first:past, AUX:])
        pair = jnp.bitwise_and(lane, HEAD // 2 - 1).astype(jnp.float32)
        angle = place.astype(jnp.float32) * jnp.exp(
            -(2.0 * pair / HEAD) * jnp.log(jnp.float32(10000.0)))
        sine = jnp.sin(angle)
        side_ref[first:past, COS:SIN] = jnp.cos(angle)
        side_ref[first:past, SIN:AUX] = jnp.where(lane < HEAD // 2, -sine, sine)
    key = turn(unit(acc[:, :HEAD], gain_ref[...]), side_ref[:, COS:SIN], side_ref[:, SIN:AUX])
    kv_ref[:, :HEAD] = key.astype(jnp.bfloat16)
    kv_ref[:, HEAD:] = acc[:, HEAD:].astype(jnp.bfloat16)


def project_keys(lens, tokens, wk, wv, gain, target):
    near, far = pl.BlockSpec(memory_space=pltpu.VMEM), pl.BlockSpec(memory_space=pltpu.HBM)
    return pl.pallas_call(
        keys_kernel,
        in_specs=[pl.BlockSpec(memory_space=pltpu.SMEM)] + [far] * 3 + [near] * 2,
        out_specs=[near] * 2,
        out_shape=[
            jax.ShapeDtypeStruct((ROWS, SIDE), jnp.float32),
            jax.ShapeDtypeStruct((ROWS, 2 * HEAD), jnp.bfloat16),
        ],
        scratch_shapes=[
            pltpu.VMEM((STEPS, ROWS, STEP), jnp.bfloat16),
            pltpu.VMEM((STEPS, STEP, 2 * HEAD), jnp.bfloat16),
            pltpu.VMEM((ROWS, 2 * HEAD), jnp.float32),
            pltpu.SemaphoreType.DMA((STEPS, 3)),
        ],
        compiler_params=pltpu.CompilerParams(vmem_limit_bytes=16 << 20),
        cost_estimate=pl.CostEstimate(
            flops=2 * ROWS * WIDTH * 256, bytes_accessed=9_500_000, transcendentals=0
        ),
        name="project_keys",
    )(lens, tokens, wk, wv, gain, target)


def queries_kernel(x_ref, wq_ref, q_ref, x_held, q_held, sems):
    part = [pl.ds(j * STEP, STEP) for j in range(STEPS)]
    copies = fetch([
        ((x_ref.at[:, part[j]], x_held.at[j]), (wq_ref.at[part[j], :], q_held.at[j]))
        for j in range(STEPS)
    ], sems)
    for j in range(STEPS):
        for copy in copies[j]:
            copy.wait()
        q = dot(x_held[j], q_held[j])
        if j == 0:
            q_ref[...] = q
        else:
            q_ref[...] += q


def project_queries(tokens, wq):
    near, far = pl.BlockSpec(memory_space=pltpu.VMEM), pl.BlockSpec(memory_space=pltpu.HBM)
    return pl.pallas_call(
        queries_kernel,
        in_specs=[far] * 2,
        out_specs=near,
        out_shape=jax.ShapeDtypeStruct((ROWS, 2 * HEAD), jnp.float32),
        scratch_shapes=[
            pltpu.VMEM((STEPS, ROWS, STEP), jnp.bfloat16),
            pltpu.VMEM((STEPS, STEP, 2 * HEAD), jnp.bfloat16),
            pltpu.SemaphoreType.DMA((STEPS, 2)),
        ],
        compiler_params=pltpu.CompilerParams(vmem_limit_bytes=16 << 20),
        cost_estimate=pl.CostEstimate(
            flops=2 * ROWS * WIDTH * 256, bytes_accessed=8_800_000, transcendentals=0
        ),
        name="project_queries",
    )(tokens, wq)


def adapt_kernel(*refs):
    rows, weights, out = refs[:X], refs[X:X + PARTS], refs[X + PARTS]
    held = refs[X + PARTS + 1]
    x, z, t = lax.axis_index("x"), lax.axis_index("z"), lax.axis_index("tp")
    for d in range(PARTS):
        for n in range(SPLIT[d]):
            held[lax.rem(z - t + T + NEAR[d] + 4 * n, T)] = weights[d][n * RANK:(n + 1) * RANK, :]
    packed = jnp.concatenate([r[...] for r in rows], axis=0)
    chunks = [(w, n * 256) for w in range(T) for n in range(PAD // 256)]
    groups = len(chunks) // 4
    left, right = [], []
    for j in range(4):
        mine = chunks[j * groups:(j + 1) * groups]
        firsts = [w * SLICE // 128 * 128 + n for w, n in mine]
        left.append(jnp.concatenate([packed[:, at:at + 256] for at in firsts], axis=1))
        right.append(jnp.concatenate([held[w, :, n:n + 256] for w, n in mine], axis=1))
    low = dot(jnp.concatenate(left, axis=0), jnp.concatenate(right, axis=0), 1, 1)
    low = sum(
        low[j * X * CAP:(j + 1) * X * CAP, j * RANK:(j + 1) * RANK] for j in range(4))
    low = low.astype(jnp.bfloat16)
    for w in range(T):
        delta = dot(low, held[w, :, PAD:]).astype(jnp.bfloat16)
        for d in range(X):
            out[lax.rem(x - d + X, X), w] = delta[d * CAP:(d + 1) * CAP, :]


def adapt(rows, weights):
    return pl.pallas_call(
        adapt_kernel,
        in_specs=[pl.BlockSpec(memory_space=pltpu.VMEM)] * (X + PARTS),
        out_specs=pl.BlockSpec(memory_space=pltpu.VMEM),
        out_shape=jax.ShapeDtypeStruct((X, T, CAP, UP), jnp.bfloat16),
        scratch_shapes=[
            pltpu.VMEM((T, RANK, PAD + UP), jnp.bfloat16),
        ],
        compiler_params=pltpu.CompilerParams(vmem_limit_bytes=12 << 20),
        cost_estimate=pl.CostEstimate(
            flops=2 * 128 * RANK * (WIDTH + 2048), bytes_accessed=3_000_000, transcendentals=0
        ),
        name="adapt",
    )(*rows, *weights)


def attend_kernel(delta_ref, q_ref, side_ref, kv0, kv1, kv2, gain_ref, out_ref, kv_ref):
    half = ROWS // TILES
    for b, source in enumerate((kv0, kv1, kv2)):
        kv_ref[b * ROWS:(b + 1) * ROWS, :2 * HEAD] = source[...]
    kv_ref[:, 2 * HEAD:] = jnp.ones((3 * ROWS, HEAD), jnp.bfloat16)
    slot = lax.broadcasted_iota(jnp.int32, (ROWS, HEAD), 1)
    column = jnp.broadcast_to(side_ref[:, SIDE - 1:].astype(jnp.int32), (ROWS, HEAD))
    chosen = jnp.concatenate(
        [(column == slot + c * HEAD).astype(jnp.float32).astype(jnp.bfloat16)
         for c in range(SLOTS // HEAD)], axis=1)
    delta = dot(chosen, delta_ref[...])
    query = q_ref[...] + delta
    gain = gain_ref[...] * (QUERY_SCALE * LOG2E)
    turned = [
        turn(unit(query[:, h * HEAD:(h + 1) * HEAD], gain), side_ref[:, COS:SIN],
             side_ref[:, SIN:AUX]).astype(jnp.bfloat16)
        for h in range(2)
    ]
    for tile in range(TILES):
        here = slice(tile * half, (tile + 1) * half)
        first, past = tile * half, tile * half + WINDOW + half
        q = jnp.concatenate([turned[0][here], turned[1][here]], axis=0)
        s = dot(q, kv_ref[first:past, :HEAD], 1, 1)
        low = side_ref[here, AUX:AUX + 1].astype(jnp.int32) - first
        at = lax.broadcasted_iota(jnp.int32, (half, WINDOW + half), 1)
        high = WINDOW + lax.broadcasted_iota(jnp.int32, (half, 1), 0)
        allowed = (at >= low) & (at <= high)
        s = jnp.where(jnp.concatenate([allowed, allowed], axis=0), s, -1e30)
        peak = jnp.max(s, axis=-1, keepdims=True)
        weights = jnp.exp2(s - peak).astype(jnp.bfloat16)
        mixed = dot(weights, kv_ref[first:past, HEAD:])
        mixed = (mixed[:, :HEAD] / mixed[:, HEAD:]).astype(jnp.bfloat16)
        out_ref[here, :HEAD] = mixed[:half]
        out_ref[here, HEAD:] = mixed[half:]


def attend(*args):
    near = pl.BlockSpec(memory_space=pltpu.VMEM)
    return pl.pallas_call(
        attend_kernel,
        in_specs=[near] * 7,
        out_specs=near,
        out_shape=jax.ShapeDtypeStruct((ROWS, 2 * HEAD), jnp.bfloat16),
        scratch_shapes=[
            pltpu.VMEM((3 * ROWS, 3 * HEAD), jnp.bfloat16),
        ],
        compiler_params=pltpu.CompilerParams(vmem_limit_bytes=24 << 20),
        cost_estimate=pl.CostEstimate(
            flops=4 * 1024 * 1280 * HEAD, bytes_accessed=4_000_000, transcendentals=1024 * 1280
        ),
        name="attend",
    )(*args)


def layer(
    tokens, query_weight, key_weight, value_weight, query_norm_gain, key_norm_gain,
    adapter_down_weight, adapter_up_weight, token_adapter_index, packed_prompt_length,
):
    down = jnp.swapaxes(adapter_down_weight[0], 0, 1)
    index, key_gain = token_adapter_index.reshape(1, ROWS), key_norm_gain.reshape(1, HEAD)
    (tokens, query_weight, key_weight, value_weight, index, key_gain, packed_prompt_length) = [
        pltpu.with_memory_space_constraint(v, pltpu.HBM)
        for v in (tokens, query_weight, key_weight, value_weight, index, key_gain,
                  packed_prompt_length)
    ]
    shift = lax.rem(lax.axis_index("tp") * SLICE, 128)
    carried = functools.reduce(
        lambda other, at: jnp.where(
            shift == at, jnp.pad(down, ((0, 0), (at, PAD + UP - SLICE - at))), other),
        (32, 64, 96), jnp.pad(down, ((0, 0), (0, PAD + UP - SLICE))))
    carried = jnp.where(
        jnp.arange(PAD + UP)[None, :] < PAD, carried,
        jnp.pad(adapter_up_weight[0], ((0, 0), (PAD, 0))))
    single, other = [
        lax.ppermute(
            carried, ("z", "tp"),
            [(a * T + w, (a + w + d) % Z * T + a) for a in range(Z) for w in range(T)])
        for d in (0, 4)
    ]
    double = jnp.concatenate([single, other], axis=0)
    weights = [double] + [
        lax.ppermute(
            double if d in (1, Z - 1) else single, "z", [((i + d) % Z, i) for i in range(Z)])
        for d in NEAR[1:]
    ]
    *rows, target = pack(index, tokens)
    rows = [rows[0]] + [
        lax.ppermute(
            rows[d], "x", [(i, (i + d) % X) for i in range(X)])
        for d in range(1, X)
    ]
    side, kv = project_keys(
        packed_prompt_length, tokens, key_weight, value_weight,
        key_gain, target)
    query = project_queries(tokens, query_weight)
    kv1, kv0 = [
        lax.ppermute(
            kv, ("x", "z"), [(i, i + d) for i in range(X * Z - d)])
        for d in (1, 2)
    ]
    delta = adapt(rows, weights)
    delta = lax.all_to_all(
        delta.reshape(X * T, CAP, UP), ("x", "tp"), 0, 0)
    return attend(
        delta.reshape(SLOTS, UP), query, side, kv0, kv1, kv, query_norm_gain.reshape(1, HEAD))


def solution(mesh):
    mesh = Mesh(mesh.devices.reshape(X, Z, T), ("x", "z", "tp"))
    seq = ("x", "z")
    in_specs = (
        P(seq, None), P(None, "tp"), P(None, "tp"), P(None, "tp"), P(), P(),
        P(seq, "tp", None), P(seq, None, "tp"), P(seq, None), P(),
    )
    return jax.shard_map(
        layer, mesh=mesh, in_specs=in_specs, out_specs=P(seq, "tp"), check_vma=False)
```

```python
import functools
import jax
import jax.numpy as jnp
from jax import lax
from jax.experimental import pallas as pl
from jax.experimental.pallas import tpu as pltpu
from jax.sharding import Mesh, PartitionSpec as P

WINDOW = 1024
QUERY_SCALE = 0.07715167498104596
LOG2E = 1.4426950408889634
TILES = 4
X, Z, T = 4, 8, 8
ROWS, WIDTH, HEAD, RANK, CAP = 512, 5376, 128, 64, 32
SLICE = WIDTH // T
PAD = 768
STEP = 768
STEPS = WIDTH // STEP
UP = 256
SLOTS = X * T * CAP
COS, SIN, AUX, SIDE = 0, HEAD, 2 * HEAD, 3 * HEAD
NEAR = (0, 1, Z - 1, 2, Z - 2)
SPLIT = (2, 2, 2, 1, 1)
PARTS = len(NEAR)


def dot(a, b, ca=1, cb=0):
    return lax.dot_general(a, b, (((ca,), (cb,)), ((), ())), preferred_element_type=jnp.float32)


def pack_kernel(idx_ref, x_ref, out0, out1, out2, out3, target_ref, held, pick, sems):
    copies = [
        pltpu.make_async_copy(x_ref.at[:, pl.ds(j * STEP, STEP)], held.at[j], sems.at[j])
        for j in range(STEPS)
    ]
    for copy in copies:
        copy.start()
    x, t = lax.axis_index("x"), lax.axis_index("tp")
    idx = idx_ref[...]
    named = lax.broadcasted_iota(jnp.int32, (X * T, ROWS), 0) == idx
    earlier = lax.broadcasted_iota(jnp.int32, (ROWS, ROWS), 0) < lax.broadcasted_iota(
        jnp.int32, (ROWS, ROWS), 1
    )
    before = dot(named.astype(jnp.float32).astype(jnp.bfloat16),
                 earlier.astype(jnp.float32).astype(jnp.bfloat16))
    rank = jnp.sum(jnp.where(named, before, 0.0), axis=0, keepdims=True).astype(jnp.int32)
    target = idx * CAP + rank
    target_ref[...] = target
    slot = lax.broadcasted_iota(jnp.int32, (CAP, ROWS), 0)
    for d in range(X):
        adapter = lax.rem(x + d, X) * T + t
        pick[d * CAP:(d + 1) * CAP, :] = (
            (slot + adapter * CAP == target).astype(jnp.float32).astype(jnp.bfloat16)
        )
    for j in range(STEPS):
        copies[j].wait()
        packed = dot(pick[...], held[j]).astype(jnp.bfloat16)
        for d, out in enumerate((out0, out1, out2, out3)):
            out[:, j * STEP:(j + 1) * STEP] = packed[d * CAP:(d + 1) * CAP, :]


def pack(idx, tokens):
    row = jax.ShapeDtypeStruct((CAP, WIDTH), jnp.bfloat16)
    return pl.pallas_call(
        pack_kernel,
        in_specs=[pl.BlockSpec(memory_space=pltpu.VMEM), pl.BlockSpec(memory_space=pltpu.HBM)],
        out_specs=[pl.BlockSpec(memory_space=pltpu.VMEM)] * (X + 2),
        out_shape=[row] * X + [
            jax.ShapeDtypeStruct((1, ROWS), jnp.int32),
            jax.ShapeDtypeStruct((STEPS, ROWS, STEP), jnp.bfloat16),
        ],
        scratch_shapes=[
            pltpu.VMEM((X * CAP, ROWS), jnp.bfloat16),
            pltpu.SemaphoreType.DMA((STEPS,)),
        ],
        cost_estimate=pl.CostEstimate(
            flops=2 * X * CAP * ROWS * WIDTH, bytes_accessed=7_000_000, transcendentals=0
        ),
        compiler_params=pltpu.CompilerParams(vmem_limit_bytes=12 << 20),
        name="pack",
    )(idx, tokens)


def unit(field, gain):
    return field / jnp.sqrt(jnp.mean(field * field, axis=-1, keepdims=True) + 1e-06) * gain


def turn(field, cosine, sine):
    return field * cosine + pltpu.roll(field, HEAD // 2, 1) * sine


def fetch(pairs, sems):
    copies = [
        [pltpu.make_async_copy(source, target, sems.at[j, n])
         for n, (source, target) in enumerate(group)]
        for j, group in enumerate(pairs)
    ]
    for group in copies:
        for copy in group:
            copy.start()
    return copies


def keys_kernel(
    lens_ref, x_held, wk_ref, wv_ref, gain_ref, target_ref, side_ref, kv_ref, kv_held, acc, sems,
):
    part = [pl.ds(j * STEP, STEP) for j in range(STEPS)]
    copies = fetch([
        ((wk_ref.at[part[j], :], kv_held.at[0, j]),
         (wv_ref.at[part[j], :], kv_held.at[1, j]))
        for j in range(STEPS)
    ], sems)
    begin = (lax.axis_index("x") * Z + lax.axis_index("z")) * ROWS
    wide = jnp.broadcast_to(target_ref[...].astype(jnp.float32), (HEAD, ROWS))
    side_ref[:, AUX:] = jnp.transpose(wide)
    lane = lax.broadcasted_iota(jnp.int32, (8, HEAD), 1)
    sign = jnp.where(lane[:1] < HEAD // 2, -1.0, 1.0)
    pair = jnp.bitwise_and(lane, HEAD // 2 - 1).astype(jnp.float32)
    freq = jnp.exp(-(2.0 * pair / HEAD) * jnp.log(jnp.float32(10000.0)))
    row = lax.broadcasted_iota(jnp.int32, (8, HEAD), 0)
    base = (begin + 64 * row).astype(jnp.float32) * freq
    base_cos, base_sin = jnp.cos(base), jnp.sin(base)
    step = lax.broadcasted_iota(jnp.int32, (64, HEAD), 0).astype(jnp.float32) * freq[:1]
    step_cos, step_sin = jnp.cos(step), jnp.sin(step)
    for j in range(STEPS):
        for copy in copies[j]:
            copy.wait()
        kv = dot(x_held[j], jnp.concatenate([kv_held[0, j], kv_held[1, j]], axis=1))
        if j == 0:
            acc[...] = kv
        else:
            acc[...] += kv
        first, past = ROWS // 8 * j // STEPS * 8, ROWS // 8 * (j + 1) // STEPS * 8
        shape = (past - first, HEAD)
        place = begin + first + lax.broadcasted_iota(jnp.int32, shape, 0)
        start = jnp.zeros(shape, jnp.int32)
        at = jnp.int32(0)
        for i in range(lens_ref.shape[0]):
            start = jnp.where(place >= at, at, start)
            at = at + lens_ref[i]
        lower = jnp.maximum(start, place - (WINDOW - 1)) - (begin - WINDOW)
        lane = lax.broadcasted_iota(jnp.int32, shape, 1)
        side_ref[first:past, AUX:] = jnp.where(
            lane < HEAD // 2, lower.astype(jnp.float32), side_ref[first:past, AUX:])
        for block in (range(8) if j == STEPS - 1 else ()):
            there = slice(block * 64, block * 64 + 64)
            c, d = base_cos[block:block + 1, :], base_sin[block:block + 1, :]
            side_ref[there, COS:SIN] = c * step_cos - d * step_sin
            side_ref[there, SIN:AUX] = sign * (d * step_cos + c * step_sin)
    key = turn(unit(acc[:, :HEAD], gain_ref[...]), side_ref[:, COS:SIN], side_ref[:, SIN:AUX])
    kv_ref[:, :HEAD] = key.astype(jnp.bfloat16)
    kv_ref[:, HEAD:] = acc[:, HEAD:].astype(jnp.bfloat16)


def project_keys(lens, tokens, wk, wv, gain, target):
    near, far = pl.BlockSpec(memory_space=pltpu.VMEM), pl.BlockSpec(memory_space=pltpu.HBM)
    return pl.pallas_call(
        keys_kernel,
        in_specs=[pl.BlockSpec(memory_space=pltpu.SMEM), near] + [far] * 2 + [near] * 2,
        out_specs=[near] * 2,
        out_shape=[
            jax.ShapeDtypeStruct((ROWS, SIDE), jnp.float32),
            jax.ShapeDtypeStruct((ROWS, 2 * HEAD), jnp.bfloat16),
        ],
        scratch_shapes=[
            pltpu.VMEM((2, STEPS, STEP, HEAD), jnp.bfloat16),
            pltpu.VMEM((ROWS, 2 * HEAD), jnp.float32),
            pltpu.SemaphoreType.DMA((STEPS, 2)),
        ],
        compiler_params=pltpu.CompilerParams(vmem_limit_bytes=16 << 20),
        cost_estimate=pl.CostEstimate(
            flops=2 * ROWS * WIDTH * 256, bytes_accessed=9_500_000, transcendentals=0
        ),
        name="project_keys",
    )(lens, tokens, wk, wv, gain, target)


def queries_kernel(x_ref, wq_ref, q_ref, x_held, q_held, sems):
    part = [pl.ds(j * STEP, STEP) for j in range(STEPS)]
    copies = fetch([
        ((x_ref.at[:, part[j]], x_held.at[j]), (wq_ref.at[part[j], :], q_held.at[j]))
        for j in range(STEPS)
    ], sems)
    for j in range(STEPS):
        for copy in copies[j]:
            copy.wait()
        q = dot(x_held[j], q_held[j])
        if j == 0:
            q_ref[...] = q
        else:
            q_ref[...] += q


def project_queries(tokens, wq):
    near, far = pl.BlockSpec(memory_space=pltpu.VMEM), pl.BlockSpec(memory_space=pltpu.HBM)
    return pl.pallas_call(
        queries_kernel,
        in_specs=[far] * 2,
        out_specs=near,
        out_shape=jax.ShapeDtypeStruct((ROWS, 2 * HEAD), jnp.float32),
        scratch_shapes=[
            pltpu.VMEM((STEPS, ROWS, STEP), jnp.bfloat16),
            pltpu.VMEM((STEPS, STEP, 2 * HEAD), jnp.bfloat16),
            pltpu.SemaphoreType.DMA((STEPS, 2)),
        ],
        compiler_params=pltpu.CompilerParams(vmem_limit_bytes=16 << 20),
        cost_estimate=pl.CostEstimate(
            flops=2 * ROWS * WIDTH * 256, bytes_accessed=8_800_000, transcendentals=0
        ),
        name="project_queries",
    )(tokens, wq)


def adapt_kernel(*refs):
    rows, weights, out = refs[:X], refs[X:X + PARTS], refs[X + PARTS]
    held = refs[X + PARTS + 1]
    x, z, t = lax.axis_index("x"), lax.axis_index("z"), lax.axis_index("tp")
    for d in range(PARTS):
        for n in range(SPLIT[d]):
            held[lax.rem(z - t + T + NEAR[d] + 4 * n, T)] = weights[d][n * RANK:(n + 1) * RANK, :]
    packed = jnp.concatenate([r[...] for r in rows], axis=0)
    chunks = [(w, n * 256) for w in range(T) for n in range(PAD // 256)]
    groups = len(chunks) // 4
    left, right = [], []
    for j in range(4):
        mine = chunks[j * groups:(j + 1) * groups]
        firsts = [w * SLICE // 128 * 128 + n for w, n in mine]
        left.append(jnp.concatenate([packed[:, at:at + 256] for at in firsts], axis=1))
        right.append(jnp.concatenate([held[w, :, n:n + 256] for w, n in mine], axis=1))
    low = dot(jnp.concatenate(left, axis=0), jnp.concatenate(right, axis=0), 1, 1)
    low = sum(
        low[j * X * CAP:(j + 1) * X * CAP, j * RANK:(j + 1) * RANK] for j in range(4))
    low = low.astype(jnp.bfloat16)
    for w in range(T):
        delta = dot(low, held[w, :, PAD:]).astype(jnp.bfloat16)
        for d in range(X):
            out[lax.rem(x - d + X, X), w] = delta[d * CAP:(d + 1) * CAP, :]


def adapt(rows, weights):
    return pl.pallas_call(
        adapt_kernel,
        in_specs=[pl.BlockSpec(memory_space=pltpu.VMEM)] * (X + PARTS),
        out_specs=pl.BlockSpec(memory_space=pltpu.VMEM),
        out_shape=jax.ShapeDtypeStruct((X, T, CAP, UP), jnp.bfloat16),
        scratch_shapes=[
            pltpu.VMEM((T, RANK, PAD + UP), jnp.bfloat16),
        ],
        compiler_params=pltpu.CompilerParams(vmem_limit_bytes=12 << 20),
        cost_estimate=pl.CostEstimate(
            flops=2 * 128 * RANK * (WIDTH + 2048), bytes_accessed=3_000_000, transcendentals=0
        ),
        name="adapt",
    )(*rows, *weights)


def attend_kernel(delta_ref, q_ref, side_ref, kv0, kv1, kv2, gain_ref, out_ref, kv_ref):
    half = ROWS // TILES
    for b, source in enumerate((kv0, kv1, kv2)):
        kv_ref[b * ROWS:(b + 1) * ROWS, :2 * HEAD] = source[...]
    kv_ref[:, 2 * HEAD:] = jnp.ones((3 * ROWS, HEAD), jnp.bfloat16)
    slot = lax.broadcasted_iota(jnp.int32, (ROWS, HEAD), 1)
    column = jnp.broadcast_to(side_ref[:, SIDE - 1:].astype(jnp.int32), (ROWS, HEAD))
    chosen = jnp.concatenate(
        [(column == slot + c * HEAD).astype(jnp.float32).astype(jnp.bfloat16)
         for c in range(SLOTS // HEAD)], axis=1)
    delta = dot(chosen, delta_ref[...])
    query = q_ref[...] + delta
    gain = gain_ref[...] * (QUERY_SCALE * LOG2E)
    turned = [
        turn(unit(query[:, h * HEAD:(h + 1) * HEAD], gain), side_ref[:, COS:SIN],
             side_ref[:, SIN:AUX]).astype(jnp.bfloat16)
        for h in range(2)
    ]
    for tile in range(TILES):
        here = slice(tile * half, (tile + 1) * half)
        first, past = tile * half, tile * half + WINDOW + half
        q = jnp.concatenate([turned[0][here], turned[1][here]], axis=0)
        s = dot(q, kv_ref[first:past, :HEAD], 1, 1)
        low = side_ref[here, AUX:AUX + 1].astype(jnp.int32) - first
        at = lax.broadcasted_iota(jnp.int32, (half, WINDOW + half), 1)
        high = WINDOW + lax.broadcasted_iota(jnp.int32, (half, 1), 0)
        allowed = (at >= low) & (at <= high)
        s = jnp.where(jnp.concatenate([allowed, allowed], axis=0), s, -1e30)
        peak = jnp.max(s, axis=-1, keepdims=True)
        weights = jnp.exp2(s - peak).astype(jnp.bfloat16)
        mixed = dot(weights, kv_ref[first:past, HEAD:])
        mixed = (mixed[:, :HEAD] / mixed[:, HEAD:]).astype(jnp.bfloat16)
        out_ref[here, :HEAD] = mixed[:half]
        out_ref[here, HEAD:] = mixed[half:]


def attend(*args):
    near = pl.BlockSpec(memory_space=pltpu.VMEM)
    return pl.pallas_call(
        attend_kernel,
        in_specs=[near] * 7,
        out_specs=near,
        out_shape=jax.ShapeDtypeStruct((ROWS, 2 * HEAD), jnp.bfloat16),
        scratch_shapes=[
            pltpu.VMEM((3 * ROWS, 3 * HEAD), jnp.bfloat16),
        ],
        compiler_params=pltpu.CompilerParams(vmem_limit_bytes=24 << 20),
        cost_estimate=pl.CostEstimate(
            flops=4 * 1024 * 1280 * HEAD, bytes_accessed=4_000_000, transcendentals=1024 * 1280
        ),
        name="attend",
    )(*args)


def layer(
    tokens, query_weight, key_weight, value_weight, query_norm_gain, key_norm_gain,
    adapter_down_weight, adapter_up_weight, token_adapter_index, packed_prompt_length,
):
    down = jnp.swapaxes(adapter_down_weight[0], 0, 1)
    index, key_gain = token_adapter_index.reshape(1, ROWS), key_norm_gain.reshape(1, HEAD)
    tokens, query_weight, key_weight, value_weight, key_gain, packed_prompt_length = [
        pltpu.with_memory_space_constraint(v, pltpu.HBM)
        for v in (tokens, query_weight, key_weight, value_weight, key_gain, packed_prompt_length)
    ]
    shift = lax.rem(lax.axis_index("tp") * SLICE, 128)
    carried = functools.reduce(
        lambda other, at: jnp.where(
            shift == at, jnp.pad(down, ((0, 0), (at, PAD + UP - SLICE - at))), other),
        (32, 64, 96), jnp.pad(down, ((0, 0), (0, PAD + UP - SLICE))))
    carried = jnp.where(
        jnp.arange(PAD + UP)[None, :] < PAD, carried,
        jnp.pad(adapter_up_weight[0], ((0, 0), (PAD, 0))))
    single, other = [
        lax.ppermute(
            carried, ("z", "tp"),
            [(a * T + w, (a + w + d) % Z * T + a) for a in range(Z) for w in range(T)])
        for d in (0, 4)
    ]
    double = jnp.concatenate([single, other], axis=0)
    weights = [double] + [
        lax.ppermute(
            double if d in (1, Z - 1) else single, "z", [((i + d) % Z, i) for i in range(Z)])
        for d in NEAR[1:]
    ]
    *rows, target, held = pack(index, tokens)
    rows = [rows[0]] + [
        lax.ppermute(
            rows[d], "x", [(i, (i + d) % X) for i in range(X)])
        for d in range(1, X)
    ]
    side, kv = project_keys(
        packed_prompt_length, held, key_weight, value_weight,
        key_gain, target)
    query = project_queries(tokens, query_weight)
    kv1, kv0 = [
        lax.ppermute(
            kv, ("x", "z"), [(i, i + d) for i in range(X * Z - d)])
        for d in (1, 2)
    ]
    delta = adapt(rows, weights)
    delta = lax.all_to_all(
        delta.reshape(X * T, CAP, UP), ("x", "tp"), 0, 0)
    return attend(
        delta.reshape(SLOTS, UP), query, side, kv0, kv1, kv, query_norm_gain.reshape(1, HEAD))


def solution(mesh):
    mesh = Mesh(mesh.devices.reshape(X, Z, T), ("x", "z", "tp"))
    seq = ("x", "z")
    in_specs = (
        P(seq, None), P(None, "tp"), P(None, "tp"), P(None, "tp"), P(), P(),
        P(seq, "tp", None), P(seq, None, "tp"), P(seq, None), P(),
    )
    return jax.shard_map(
        layer, mesh=mesh, in_specs=in_specs, out_specs=P(seq, "tp"), check_vma=False)
```
